32 devices in a mesh: dp: 4 (over y, core), row: 2 (over x), col: 4 (over z).
Axes of the slice: x: 2, y: 2, z: 4, core: 2. Of those that a mesh axis runs over, the one named last changes fastest.
Arguments:
- tokens: bfloat16 [2048, 1024], P(('dp', 'row'), 'col'), may hold values from -6 to 6
- segment_index: int32 [4, 512], P('dp'), may hold values from 0 to 1, as said below
- cotangent: bfloat16 [2048, 1024], P(('dp', 'row'), 'col'), may hold values from -6 to 6
- norm_gain: float32 [2, 1024], P(None, 'col'), may hold values from 0.25 to 1.75
- gate_weight: bfloat16 [2, 1024, 2048], P(None, 'row', 'col'), may hold values from -0.1875 to 0.1875
- inner_weight: bfloat16 [2, 1024, 2048], P(None, 'row', 'col'), may hold values from -0.1875 to 0.1875
- state_weight: bfloat16 [2, 1024, 256], P(None, 'row'), may hold values from -0.1875 to 0.1875
- step_weight: bfloat16 [2, 1024, 32], P(None, 'row', 'col'), may hold values from -0.1875 to 0.1875
- inner_kernel: float32 [2, 2048, 4], P(None, 'col'), may hold values from -3 to 3
- inner_bias: float32 [2, 2048], P(None, 'col'), may hold values from -0.5 to 0.5
- state_kernel: float32 [2, 256, 4], replicated, may hold values from -3 to 3
- state_bias: float32 [2, 256], replicated, may hold values from -0.5 to 0.5
- step_bias: float32 [2, 32], P(None, 'col'), may hold values from -4 to -1
- decay_log: float32 [2, 32], P(None, 'col'), may hold values from -6.5 to 0.5
- skip_gain: float32 [2, 32], P(None, 'col'), may hold values from 0.5 to 1.5
- gated_gain: float32 [2, 2048], P(None, 'col'), may hold values from 0.25 to 1.75
- output_weight: bfloat16 [2, 2048, 1024], P(None, 'col', 'row'), may hold values from -0.125 to 0.125
Outputs:
- layer_output: bfloat16 [2048, 1024], P(('dp', 'row'), 'col')
- input_grad: float32 [2048, 1024], P(('dp', 'row'), 'col')
- norm_gain_grad: float32 [2, 1024], P(None, 'col')
- gate_weight_grad: float32 [2, 1024, 2048], P(None, ('dp', 'row'), 'col')
- inner_weight_grad: float32 [2, 1024, 2048], P(None, ('dp', 'row'), 'col')
- state_weight_grad: float32 [2, 1024, 256], P(None, ('dp', 'row'), 'col')
- step_weight_grad: float32 [2, 1024, 32], P(None, ('dp', 'row'), 'col')
- inner_kernel_grad: float32 [2, 2048, 4], P(None, 'col')
- inner_bias_grad: float32 [2, 2048], P(None, 'col')
- state_kernel_grad: float32 [2, 256, 4], P(None, 'col')
- state_bias_grad: float32 [2, 256], P(None, 'col')
- step_bias_grad: float32 [2, 32], P(None, 'col')
- decay_log_grad: float32 [2, 32], P(None, 'col')
- skip_gain_grad: float32 [2, 32], P(None, 'col')
- gated_gain_grad: float32 [2, 2048], P(None, 'col')
- output_weight_grad: float32 [2, 2048, 1024], P(None, 'col', ('dp', 'row'))
The draws below stay inside these ranges and needn't reach their ends.
Inputs may be any that keep to these rules, and one draw needn't show every extreme that they name: `segment_index`: each row is one group of 512 tokens holding two sequences: 0 up to a boundary, 1 from it on; each sequence has at least 2048 tokens, or a quarter of 512 where that is fewer.
All inputs are finite; a program needn't handle non-finite values.
Results may differ from the reference program's by a relative error of at most 0.0085.
The reference program's roundings to bfloat16 on the way count: a program that leaves them out, or rounds other values in their place, can miss the bound.
Values may be sent and summed in bfloat16 or wider, within the bound.
A program may use at most 128 MiB of HBM per device.

```python
import jax
import jax.numpy as jnp
from jax import lax

D = 1024
INNER = 2048
HEADS = 32
HEAD_DIM = 64
STATE = 128
KERNEL = 4
SPAN = 256
LAYERS = 2
SEQ_MIN = 2048
TOK_GROUP = 512
GROUPS = 4
TOKENS = 2048


def draw_segment_index(key, part):
    lowest = min(SEQ_MIN, TOK_GROUP // 4)
    cuts = jax.random.randint(key, (GROUPS, 1), lowest, TOK_GROUP - lowest + 1)
    places = jnp.arange(TOK_GROUP, dtype=jnp.int32)[None, :]
    return (places >= cuts).astype(jnp.int32)


def block_levels(own_key, shape, split, smallest, top_value):
    factor_of, own = 1.0, jax.random.fold_in(own_key, 6)
    for dim, blocks in split:
        steps = jnp.exp(jax.random.uniform(jax.random.fold_in(own, dim), (blocks,), jnp.float32, smallest / len(split), top_value / len(split)))
        factor_of = factor_of * jnp.repeat(steps, shape[dim] // blocks).reshape([-1 if axis == dim else 1 for axis in range(len(shape))])
    return factor_of


def scatter_about(key, shape, scale, reach, cuts=(), kind=jnp.bfloat16):
    values = scale * jax.random.normal(key, shape, jnp.float32)
    if cuts:
        values = values * block_levels(key, shape, cuts, -0.22, 0.18)
    return jnp.clip(values, -reach, reach).astype(kind)


def setup_inputs(seed: int = 0) -> dict:
    splits = jax.random.split(jax.random.key(seed), 18)
    return {
        "tokens": scatter_about(splits[0], (TOKENS, D), 1.0, 6.0, ((0, 8), (1, 4))),
        "segment_index": draw_segment_index(jax.random.fold_in(splits[17], 71), 0),
        "cotangent": scatter_about(splits[2], (TOKENS, D), 1.0, 6.0, ((0, 8), (1, 4))),
        "norm_gain": jnp.clip(1.0 + 0.15 * jax.random.normal(splits[3], (LAYERS, D), jnp.float32), 0.25, 1.75),
        "gate_weight": scatter_about(splits[4], (LAYERS, D, INNER), D ** -0.5, 0.1875, ((1, 2), (2, 4))),
        "inner_weight": scatter_about(splits[5], (LAYERS, D, INNER), D ** -0.5, 0.1875, ((1, 2), (2, 4))),
        "state_weight": scatter_about(splits[6], (LAYERS, D, 2 * STATE), D ** -0.5, 0.1875, ((1, 2),)),
        "step_weight": scatter_about(splits[7], (LAYERS, D, HEADS), D ** -0.5, 0.1875, ((1, 2), (2, 4))),
        "inner_kernel": scatter_about(splits[8], (LAYERS, INNER, KERNEL), KERNEL ** -0.5, 3.0, ((1, 4),), jnp.float32),
        "inner_bias": jnp.clip(jax.random.uniform(splits[9], (LAYERS, INNER), jnp.float32, -0.5, 0.5) * block_levels(splits[9], (LAYERS, INNER), ((1, 4),), -0.4, 0.0), -0.5, 0.5),
        "state_kernel": scatter_about(splits[10], (LAYERS, 2 * STATE, KERNEL), KERNEL ** -0.5, 3.0, (), jnp.float32),
        "state_bias": jnp.clip(jax.random.uniform(splits[11], (LAYERS, 2 * STATE), jnp.float32, -0.5, 0.5), -0.5, 0.5),
        "step_bias": jnp.clip(-4.0 + 3.0 * jax.random.uniform(splits[12], (LAYERS, HEADS), jnp.float32) ** block_levels(splits[12], (LAYERS, HEADS), ((1, 4),), -0.2, 0.2), -4.0, -1.0),
        "decay_log": jnp.clip(-6.5 + 7.0 * jax.random.uniform(splits[13], (LAYERS, HEADS), jnp.float32) ** block_levels(splits[13], (LAYERS, HEADS), ((1, 4),), -0.2, 0.2), -6.5, 0.5),
        "skip_gain": jnp.clip(0.5 + 1.0 * jax.random.uniform(splits[14], (LAYERS, HEADS), jnp.float32) ** block_levels(splits[14], (LAYERS, HEADS), ((1, 4),), -0.2, 0.2), 0.5, 1.5),
        "gated_gain": jnp.clip(1.0 + 0.15 * jax.random.normal(splits[15], (LAYERS, INNER), jnp.float32), 0.25, 1.75),
        "output_weight": scatter_about(splits[16], (LAYERS, INNER, D), INNER ** -0.5, 0.125, ((1, 4), (2, 2))),
    }


EPSILON = 1e-05
HIGHEST = lax.Precision.HIGHEST

@jax.custom_vjp
def low(v):
    return lax.optimization_barrier(v.astype(jnp.bfloat16)).astype(jnp.float32)

@jax.custom_vjp
def low_back(v):
    return v

def low_keep(v):
    return (low(v), None)

def low_pass(kept, grad):
    return (grad,)

def back_keep(v):
    return (v, None)

def back_low(kept, grad):
    return (low(grad),)
low.defvjp(low_keep, low_pass)
low_back.defvjp(back_keep, back_low)

def matmul(lhs_mat, rhs_mat):
    return jnp.dot(lhs_mat, rhs_mat, precision=HIGHEST, preferred_element_type=jnp.float32)

def rms_scale(values, gain_row):
    return values * lax.rsqrt(lax.optimization_barrier(jnp.mean(values * values, axis=-1, keepdims=True)) + EPSILON) * gain_row

def causal_conv(values, kernel, bias_row, segments):
    tok_count = values.shape[0]
    padded = jnp.concatenate([jnp.zeros((KERNEL - 1, values.shape[1]), jnp.float32), values], axis=0)
    seg_pad = jnp.concatenate([jnp.full((KERNEL - 1,), -1, jnp.int32), segments.astype(jnp.int32)])
    summed = jnp.zeros_like(values) + bias_row[None, :]
    for offset in range(KERNEL):
        same_seq = (seg_pad[offset:offset + tok_count] == segments).astype(jnp.float32)
        summed = summed + kernel[:, offset][None, :] * padded[offset:offset + tok_count] * same_seq[:, None]
    return jax.nn.silu(summed)

def block_step(state_now, pieces):
    xs_block, dt_block, decay_block, b_block, c_block, seg_block, seg_prior = pieces
    cumulative = jnp.cumsum(decay_block, axis=0)
    places = jnp.arange(SPAN)
    same_seq = (seg_block[:, None] == seg_block[None, :]) & (places[:, None] >= places[None, :])
    spread = cumulative[:, None, :] - cumulative[None, :, :]
    mixing = jnp.exp(jnp.where(same_seq[:, :, None], spread, -60.0)) * same_seq[:, :, None].astype(jnp.float32)
    scores = jnp.dot(c_block, b_block.T, precision=HIGHEST)
    weights = mixing * scores[:, :, None] * dt_block[None, :, :]
    intra_part = jnp.einsum('ijh,jhp->ihp', weights, xs_block, precision=HIGHEST)
    entry_gate = jnp.exp(cumulative) * (seg_block == seg_prior).astype(jnp.float32)[:, None]
    incoming = jnp.einsum('hpn,in->ihp', state_now, c_block, precision=HIGHEST)
    tail_gate = jnp.exp(cumulative[-1][None, :] - cumulative) * (seg_block == seg_block[-1]).astype(jnp.float32)[:, None] * dt_block
    block_decay = jnp.exp(cumulative[-1]) * (seg_block[-1] == seg_prior).astype(jnp.float32)
    fresh_state = jnp.einsum('jh,jhp,jn->hpn', tail_gate, xs_block, b_block, precision=HIGHEST)
    new_state = block_decay[:, None, None] * state_now + fresh_state
    return (new_state, intra_part + entry_gate[:, :, None] * incoming)

def mixer_layer(resid, segments, layer_params):
    norm_gain, gate_weight, inner_weight, state_weight, step_weight, inner_kernel, inner_bias, state_kernel, state_bias, step_bias, decay_log, skip_gain, gated_gain, output_weight = layer_params
    tok_count = resid.shape[0]
    block_count = tok_count // SPAN
    normed = low(rms_scale(resid, norm_gain))
    gate_val = low_back(matmul(normed, gate_weight))
    inner_val = low_back(matmul(normed, inner_weight))
    pair_val = low_back(matmul(normed, state_weight))
    raw_step = low_back(matmul(normed, step_weight))
    xs_all = causal_conv(inner_val, inner_kernel, inner_bias, segments).reshape(tok_count, HEADS, HEAD_DIM)
    pair_post = causal_conv(pair_val, state_kernel, state_bias, segments)
    b_all = pair_post[:, :STATE]
    c_all = pair_post[:, STATE:]
    step_size = jax.nn.softplus(raw_step + step_bias[None, :])
    decay_now = -jnp.exp(decay_log)[None, :] * step_size
    seg_prior = jnp.concatenate([jnp.full((1,), -1, jnp.int32), segments[SPAN - 1:-1:SPAN]])

    def shape_blocks(values):
        return values.reshape((block_count, SPAN) + values.shape[1:])
    start_state = jnp.zeros((HEADS, HEAD_DIM, STATE), jnp.float32)
    unused, mixed_ssd = lax.scan(jax.checkpoint(block_step), start_state, (shape_blocks(xs_all), shape_blocks(step_size), shape_blocks(decay_now), shape_blocks(b_all), shape_blocks(c_all), shape_blocks(segments), seg_prior))
    ssd_out = mixed_ssd.reshape(tok_count, HEADS, HEAD_DIM) + skip_gain[None, :, None] * xs_all
    gated = ssd_out.reshape(tok_count, INNER) * jax.nn.silu(gate_val)
    normed_y = low(rms_scale(gated, gated_gain))
    branch = low_back(matmul(normed_y, output_weight))
    return resid + branch

def reference(tokens, segment_index, cotangent, norm_gain, gate_weight, inner_weight, state_weight, step_weight, inner_kernel, inner_bias, state_kernel, state_bias, step_bias, decay_log, skip_gain, gated_gain, output_weight):
    params = tuple((param.astype(jnp.float32) for param in (norm_gain, gate_weight, inner_weight, state_weight, step_weight, inner_kernel, inner_bias, state_kernel, state_bias, step_bias, decay_log, skip_gain, gated_gain, output_weight)))
    inputs = tokens.astype(jnp.float32).reshape(GROUPS, TOK_GROUP, D)
    cot_all = cotangent.astype(jnp.float32).reshape(GROUPS, TOK_GROUP, D)

    def one_group(totals, element):
        group_in, group_seg, group_cot = element

        def forward(start_val, weights):
            resid = start_val
            for layer_at in range(LAYERS):
                resid = mixer_layer(resid, group_seg, tuple((w_all[layer_at] for w_all in weights)))
            return resid
        result, pullback = jax.vjp(forward, group_in, params)
        grad_in, grad_params = pullback(group_cot)
        totals = tuple((old_sum + new_term for old_sum, new_term in zip(totals, grad_params)))
        return (totals, (result, grad_in))
    zeros_all = tuple((jnp.zeros_like(param) for param in params))
    grads, outputs = lax.scan(one_group, zeros_all, (inputs, segment_index, cot_all))
    layer_output = outputs[0].reshape(TOKENS, D).astype(jnp.bfloat16)
    input_grad = outputs[1].reshape(TOKENS, D)
    return (layer_output, input_grad, grads[0], grads[1], grads[2], grads[3], grads[4], grads[5], grads[6], grads[7], grads[8], grads[9], grads[10], grads[11], grads[12], grads[13])
```

```python
import functools

import jax
import jax.numpy as jnp
from jax import lax
from jax.experimental import pallas as pl
from jax.experimental.pallas import tpu as pltpu
from jax.sharding import PartitionSpec as P

KERNEL = 4
SPAN = 256
LAYERS = 2


EPSILON = 1e-05
HIGHEST = lax.Precision.HIGHEST


def passed_along(value, axis, by):
    devices = lax.axis_size(axis)
    pairs = [(i, i + by) for i in range(devices) if 0 <= i + by < devices]
    return lax.ppermute(value, axis, pairs)


def carried_in(part, axis, combine, identity, reverse):
    count = lax.axis_size(axis)
    place = lax.axis_index(axis)
    if count == 2:
        moved = lax.ppermute(part[1], axis, [(1, 0)] if reverse else [(0, 1)])
        return (None, moved)
    ahead = count - 1 - place if reverse else place
    gathered = jax.tree.map(lambda a: lax.all_gather(a, axis), part)
    state = jax.tree.map(lambda a, e: jnp.zeros_like(a) + jnp.asarray(e, a.dtype), part, identity)

    def one(turn, state):
        source = count - 1 - turn if reverse else turn
        return combine(
            state, jax.tree.map(lambda a: lax.dynamic_index_in_dim(a, source, 0, False), gathered)
        )

    return lax.fori_loop(0, ahead, one, state)


MESH = pl.DeviceIdType.MESH
VMEM_SPEC = pl.BlockSpec(memory_space=pltpu.VMEM)
ANY_SPEC = pl.BlockSpec(memory_space=pl.ANY)


def greet(peers):
    barrier = pltpu.get_barrier_semaphore()
    for peer in peers:
        pl.semaphore_signal(barrier, inc=1, device_id=peer, device_id_type=MESH)
    pl.semaphore_wait(barrier, len(peers))


def col_peers(n):
    me = lax.axis_index("col")
    return [{"col": lax.rem(me + k, n)} for k in range(1, n)]


def start_to(peers, src_of, dst, send, recv):
    copies = []
    for k, peer in enumerate(peers):
        copy = pltpu.make_async_remote_copy(
            src_ref=src_of(peer),
            dst_ref=dst,
            send_sem=send.at[k],
            recv_sem=recv.at[k],
            device_id=peer,
            device_id_type=MESH,
        )
        copy.start()
        copies.append(copy)
    return copies


def row_sum_kernel(n, value_ref, total_ref, slots, send, recv):
    me = lax.axis_index("col")
    peers = col_peers(n)
    slots[me] = value_ref[...]
    greet(peers)
    copies = start_to(peers, lambda peer: value_ref, slots.at[me], send, recv)
    for copy in copies:
        copy.wait()
    total = slots[0]
    for k in range(1, n):
        total = total + slots[k]
    total_ref[...] = total


def row_total(values):
    n = lax.axis_size("col")
    rows = values.shape[0]
    out = pl.pallas_call(
        functools.partial(row_sum_kernel, n),
        out_shape=jax.ShapeDtypeStruct((1, rows), jnp.float32),
        in_specs=[VMEM_SPEC],
        out_specs=VMEM_SPEC,
        scratch_shapes=[
            pltpu.VMEM((n, 1, rows), jnp.float32),
            pltpu.SemaphoreType.DMA((n - 1,)),
            pltpu.SemaphoreType.DMA((n - 1,)),
        ],
        compiler_params=pltpu.CompilerParams(collective_id=0, has_side_effects=True),
        name="row_total",
    )(values.reshape(1, rows))
    return out[0]


def scatter_sum(n, part_ref, outgoing, arrived, send, recv):
    me = lax.axis_index("col")
    peers = col_peers(n)
    width = outgoing.shape[2]
    for k in range(n):
        outgoing[k] = part_ref[:, k * width : (k + 1) * width].astype(outgoing.dtype)
    greet(peers)
    copies = start_to(peers, lambda peer: outgoing.at[peer["col"]], arrived.at[me], send, recv)
    total = part_ref[:, pl.ds(pl.multiple_of(me * width, width), width)]
    for copy in copies:
        copy.wait()
    for peer in peers:
        total = total + arrived[peer["col"]].astype(jnp.float32)
    return total


def rows_over_col(n, product, row_own, row_slots, send, recv):
    me = lax.axis_index("col")
    peers = col_peers(n)
    ones = jnp.ones((8, product.shape[1]), jnp.float32)
    sums = lax.dot_general(
        ones, product, (((1,), (1,)), ((), ())), precision=HIGHEST,
        preferred_element_type=jnp.float32,
    )
    row_own[...] = sums
    row_slots[me] = sums
    copies = start_to(peers, lambda peer: row_own, row_slots.at[me], send, recv)
    for copy in copies:
        copy.wait()
    total = row_slots[0]
    for k in range(1, n):
        total = total + row_slots[k]
    return jnp.transpose(total)[:, :1]


def gather_cols(n, own, all_ref, send, recv):
    me = lax.axis_index("col")
    peers = col_peers(n)
    width = own.shape[1]
    place = all_ref.at[:, pl.ds(pl.multiple_of(me * width, width), width)]
    place[...] = own[...]
    copies = start_to(peers, lambda peer: own, place, send, recv)
    for copy in copies:
        copy.wait()


def forward_turn_kernel(
    n, part_ref, resid_ref, gain_ref, resid_out, scale_out, normed_out,
    outgoing, arrived, row_own, row_slots, own, *sems,
):
    resid = resid_ref[...] + scatter_sum(n, part_ref, outgoing, arrived, sems[0], sems[1])
    resid_out[...] = resid
    square = rows_over_col(n, resid * resid, row_own, row_slots, sems[2], sems[3])
    scale = lax.rsqrt(square / (n * resid.shape[1]) + EPSILON)
    scale_out[...] = scale
    own[...] = (resid * scale * gain_ref[...]).astype(jnp.bfloat16)
    gather_cols(n, own, normed_out, sems[4], sems[5])


def backward_turn_kernel(
    n, spread, part_ref, grad_ref, resid_ref, scale_ref, gain_ref, grad_out, gain_out, *rest
):
    if spread:
        cot_out, rest = rest[0], rest[1:]
    outgoing, arrived, row_own, row_slots, own = rest[:5]
    sems = rest[5:]
    d_normed = scatter_sum(n, part_ref, outgoing, arrived, sems[0], sems[1])
    resid = resid_ref[...]
    scale = scale_ref[...]
    scaled_in = d_normed * gain_ref[...]
    gain_out[...] = jnp.sum(d_normed * resid * scale, axis=0, keepdims=True)
    total = rows_over_col(n, scaled_in * resid, row_own, row_slots, sems[2], sems[3])
    grad = (
        grad_ref[...]
        + scale * scaled_in
        - resid * (scale * scale * scale * total / (n * resid.shape[1]))
    )
    grad_out[...] = grad
    if spread:
        own[...] = grad.astype(jnp.bfloat16)
        gather_cols(n, own, cot_out, sems[4], sems[5])


def turn_scratch(n, rows, width):
    return [
        pltpu.VMEM((n, rows, width), jnp.bfloat16),
        pltpu.VMEM((n, rows, width), jnp.bfloat16),
        pltpu.VMEM((8, rows), jnp.float32),
        pltpu.VMEM((n, 8, rows), jnp.float32),
        pltpu.VMEM((rows, width), jnp.bfloat16),
    ] + [pltpu.SemaphoreType.DMA((n - 1,)) for _ in range(6)]


def forward_turn(part, resid, gain):
    n = lax.axis_size("col")
    rows, width = resid.shape
    return pl.pallas_call(
        functools.partial(forward_turn_kernel, n),
        out_shape=[
            jax.ShapeDtypeStruct((rows, width), jnp.float32),
            jax.ShapeDtypeStruct((rows, 1), jnp.float32),
            jax.ShapeDtypeStruct((rows, n * width), jnp.bfloat16),
        ],
        in_specs=[VMEM_SPEC] * 3,
        out_specs=[VMEM_SPEC] * 3,
        scratch_shapes=turn_scratch(n, rows, width),
        compiler_params=pltpu.CompilerParams(collective_id=1, has_side_effects=True),
        name="forward_turn",
    )(part, resid, gain[None, :])


def backward_turn(part, grad, resid, scale, gain, spread):
    n = lax.axis_size("col")
    rows, width = resid.shape
    outs = [
        jax.ShapeDtypeStruct((rows, width), jnp.float32),
        jax.ShapeDtypeStruct((1, width), jnp.float32),
    ]
    if spread:
        outs.append(jax.ShapeDtypeStruct((rows, n * width), jnp.bfloat16))
    return pl.pallas_call(
        functools.partial(backward_turn_kernel, n, spread),
        out_shape=outs,
        in_specs=[VMEM_SPEC] * 5,
        out_specs=[VMEM_SPEC] * len(outs),
        scratch_shapes=turn_scratch(n, rows, width),
        compiler_params=pltpu.CompilerParams(
            collective_id=2 if spread else 3, has_side_effects=True
        ),
        name="backward_turn" if spread else "backward_end",
    )(part, grad, resid, scale[:, None], gain[None, :])


def entry_kernel(n, tok_ref, gain_ref, tok_all, gain_all, *sems):
    me = lax.axis_index("col")
    peers = col_peers(n)
    width = tok_ref.shape[1]
    place = tok_all.at[:, pl.ds(pl.multiple_of(me * width, width), width)]
    place[...] = tok_ref[...]
    gain_all[me] = gain_ref[...]
    greet(peers)
    copies = start_to(peers, lambda peer: tok_ref, place, sems[0], sems[1])
    copies += start_to(peers, lambda peer: gain_ref, gain_all.at[me], sems[2], sems[3])
    for copy in copies:
        copy.wait()


def entry_gather(tokens, gain):
    n = lax.axis_size("col")
    rows, width = tokens.shape
    return pl.pallas_call(
        functools.partial(entry_kernel, n),
        out_shape=[
            jax.ShapeDtypeStruct((rows, n * width), tokens.dtype),
            jax.ShapeDtypeStruct((n, 1, width), gain.dtype),
        ],
        in_specs=[VMEM_SPEC] * 2,
        out_specs=[VMEM_SPEC] * 2,
        scratch_shapes=[pltpu.SemaphoreType.DMA((n - 1,)) for _ in range(4)],
        compiler_params=pltpu.CompilerParams(collective_id=4, has_side_effects=True),
        name="entry_gather",
    )(tokens, gain[None, :])


def small_kernel(dp, row, value_ref, total_ref, slots, send, recv):
    at_dp, at_row = lax.axis_index("dp"), lax.axis_index("row")
    me = at_dp * row + at_row
    peers = []
    for k in range(1, dp * row):
        peers.append(
            {"dp": lax.rem(at_dp + k // row, dp), "row": lax.rem(at_row + k % row, row)}
        )
    slots[me] = value_ref[...]
    greet(peers)
    copies = start_to(peers, lambda peer: value_ref, slots.at[me], send, recv)
    for copy in copies:
        copy.wait()
    total = slots[0]
    for k in range(1, dp * row):
        total = total + slots[k]
    total_ref[...] = total


def small_total(value):
    dp, row = lax.axis_size("dp"), lax.axis_size("row")
    count = dp * row
    if count > 8:
        return lax.psum(value, ("dp", "row"))
    return pl.pallas_call(
        functools.partial(small_kernel, dp, row),
        out_shape=jax.ShapeDtypeStruct(value.shape, jnp.float32),
        in_specs=[VMEM_SPEC],
        out_specs=VMEM_SPEC,
        scratch_shapes=[
            pltpu.VMEM((count,) + value.shape, jnp.float32),
            pltpu.SemaphoreType.DMA((count - 1,)),
            pltpu.SemaphoreType.DMA((count - 1,)),
        ],
        compiler_params=pltpu.CompilerParams(collective_id=5, has_side_effects=True),
        name="small_total",
    )(value)


def whole_over_row(block, axis):
    if lax.axis_size("row") != 2:
        return lax.all_gather(block, "row", axis=axis, tiled=True)
    other = lax.ppermute(block, "row", [(0, 1), (1, 0)])
    size = block.shape[axis]
    trio = jnp.concatenate([block, other, block], axis=axis)
    return lax.dynamic_slice_in_dim(trio, lax.axis_index("row") * size, 2 * size, axis)


def whole_over_col(block):
    n = lax.axis_size("col")
    size = block.shape[1]
    blocks = [block]
    for k in range(1, n):
        blocks.append(lax.ppermute(block, "col", [(i, (i - k) % n) for i in range(n)]))
    twice = jnp.concatenate(blocks + blocks[:-1], axis=1)
    start = lax.rem(n - lax.axis_index("col"), n) * size
    return lax.dynamic_slice_in_dim(twice, start, n * size, 1)


def packed_small(parts):
    flat = jnp.concatenate([part.reshape(-1) for part in parts])
    total = flat.shape[0]
    lines = -(-total // 1024) * 8
    return jnp.pad(flat, (0, lines * 128 - total)).reshape(lines, 128)


def unpacked_small(packed, shapes):
    flat = packed.reshape(-1)
    out, at = [], 0
    for shape in shapes:
        size = 1
        for extent in shape:
            size *= extent
        out.append(flat[at : at + size].reshape(shape))
        at += size
    return out


def link_up(earlier, later):
    return (earlier[0] * later[0], later[0][:, None, None] * earlier[1] + later[1])


def link_down(earlier, later):
    return (earlier[0] * later[0], later[1] + later[0][:, None, None] * earlier[1])


def mixer_parts(
    post_x, b_mat, c_mat, raw_step, step_off, decay_rate, skip_rate, segments, seg_prior
):
    tok_count = post_x.shape[0]
    head_count = raw_step.shape[1]
    head_width = post_x.shape[1] // head_count
    block_count = tok_count // SPAN
    step_size = jax.nn.softplus(raw_step + step_off[None, :])
    decay_now = -jnp.exp(decay_rate)[None, :] * step_size
    xs_c = post_x.reshape(block_count, SPAN, head_count, head_width)
    step_c = step_size.reshape(block_count, SPAN, head_count)
    cumulative = jnp.cumsum(decay_now.reshape(block_count, SPAN, head_count), axis=1)
    b_c = b_mat.reshape(block_count, SPAN, -1)
    c_c = c_mat.reshape(block_count, SPAN, -1)
    seg_c = segments.reshape(block_count, SPAN)
    places = jnp.arange(SPAN)
    same_seq = (seg_c[:, :, None] == seg_c[:, None, :]) & (places[:, None] >= places[None, :])[None]
    causal = same_seq.astype(jnp.float32)[:, None, :, :]
    cum_heads = jnp.transpose(cumulative, (0, 2, 1))
    step_heads = jnp.transpose(step_c, (0, 2, 1))
    spread = cum_heads[:, :, :, None] - cum_heads[:, :, None, :]
    scores = jnp.einsum("cin,cjn->cij", c_c, b_c, precision=HIGHEST)
    weights = jnp.exp(spread * causal) * causal * scores[:, None, :, :] * step_heads[:, :, None, :]
    intra_part = jnp.einsum("chij,cjhp->cihp", weights, xs_c, precision=HIGHEST)
    entry_gate = jnp.exp(cumulative) * (seg_c == seg_prior[:, None]).astype(jnp.float32)[..., None]
    tail_gate = (
        jnp.exp(cumulative[:, -1:, :] - cumulative)
        * (seg_c == seg_c[:, -1:]).astype(jnp.float32)[..., None]
        * step_c
    )
    fresh_state = jnp.einsum("cjh,cjhp,cjn->chpn", tail_gate, xs_c, b_c, precision=HIGHEST)
    block_decay = (
        jnp.exp(cumulative[:, -1, :]) * (seg_c[:, -1] == seg_prior).astype(jnp.float32)[:, None]
    )

    def advance(state_now, element):
        return (element[1][:, None, None] * state_now + element[0], state_now)

    dev_state, starts = lax.scan(
        advance, jnp.zeros_like(fresh_state[0]), (fresh_state, block_decay)
    )
    prefix = jnp.cumprod(
        jnp.concatenate([jnp.ones_like(block_decay), block_decay[:-1]], axis=0), axis=0
    )
    dev_decay = prefix[-1] * block_decay[-1]
    local_part = intra_part + skip_rate[None, None, :, None] * xs_c
    return (local_part, entry_gate, c_c, starts, prefix, dev_state, dev_decay)


def mixer_finish(pieces, entry_state):
    local_part, entry_gate, c_c, starts, prefix, dev_state, dev_decay = pieces
    states = starts + prefix[:, :, None, None] * entry_state[None]
    incoming = jnp.einsum("chpn,cin->cihp", states, c_c, precision=HIGHEST)
    mixed_out = local_part + entry_gate[..., None] * incoming
    return mixed_out.reshape(mixed_out.shape[0] * SPAN, -1)


def mixer_core(
    post_x,
    b_mat,
    c_mat,
    raw_step,
    step_off,
    decay_rate,
    skip_rate,
    entry_state,
    segments,
    seg_prior,
):
    pieces = mixer_parts(
        post_x, b_mat, c_mat, raw_step, step_off, decay_rate, skip_rate, segments, seg_prior
    )
    return (mixer_finish(pieces, entry_state), pieces[5], pieces[6])


def local(
    tokens,
    segment_index,
    cotangent,
    norm_gain,
    gate_weight,
    inner_weight,
    state_weight,
    step_weight,
    inner_kernel,
    inner_bias,
    state_kernel,
    state_bias,
    step_bias,
    decay_log,
    skip_gain,
    gated_gain,
    output_weight,
):
    tok_rows = tokens.shape[0]
    full_width = tokens.shape[1] * lax.axis_size("col")
    head_count = step_bias.shape[1]
    inner_cols = inner_kernel.shape[1]
    inner_full = inner_cols * lax.axis_size("col")
    state_cols = state_kernel.shape[1]
    state_half = state_cols // 2
    share_cols = state_cols // lax.axis_size("col")
    col_at = lax.axis_index("col")
    first_tok = lax.axis_index("row") * tok_rows
    group_seg = segment_index[0]
    seg_front = jnp.concatenate([jnp.full((KERNEL - 1,), -1, jnp.int32), group_seg])
    seg_rear = jnp.concatenate([group_seg, jnp.full((KERNEL - 1,), -2, jnp.int32)])
    seg_early = lax.dynamic_slice_in_dim(seg_front, first_tok, tok_rows + KERNEL - 1)
    seg_late = lax.dynamic_slice_in_dim(seg_rear, first_tok, tok_rows + KERNEL - 1)
    segments = seg_early[KERNEL - 1 :]
    seg_prior = jnp.concatenate(
        [seg_early[KERNEL - 2 : KERNEL - 1], segments[SPAN - 1 : -1 : SPAN]]
    )
    dims_t = (((1,), (1,)), ((), ()))
    dims_w = (((0,), (0,)), ((), ()))
    resid = tokens.astype(jnp.float32)
    tokens_all, gain_all = entry_gather(tokens, norm_gain[0])
    first_all = tokens_all.astype(jnp.float32)
    row_scale = lax.rsqrt(jnp.sum(first_all * first_all, axis=1) / full_width + EPSILON)
    normed_all = (first_all * row_scale[:, None] * gain_all.reshape(1, -1)).astype(jnp.bfloat16)
    whole_weights = [
        (
            whole_over_row(gate_weight[layer_at], 0),
            whole_over_row(inner_weight[layer_at], 0),
            whole_over_row(state_weight[layer_at], 0),
            whole_over_row(step_weight[layer_at], 0),
            whole_over_row(output_weight[layer_at], 1),
        )
        for layer_at in range(LAYERS)
    ]
    cot_all = whole_over_col(cotangent)
    saved = []
    for layer_at in range(LAYERS):
        gate_full, inner_whole, state_full, step_full, output_full = whole_weights[layer_at]
        gate_val = jnp.dot(normed_all, gate_full, preferred_element_type=jnp.float32)
        inner_val = jnp.dot(normed_all, inner_whole, preferred_element_type=jnp.float32)
        pair_val = jnp.dot(normed_all, state_full, preferred_element_type=jnp.float32)
        raw_step = jnp.dot(normed_all, step_full, preferred_element_type=jnp.float32)
        values = jnp.concatenate([inner_val, pair_val], axis=1)
        before = passed_along(values[tok_rows - (KERNEL - 1) :], "row", 1)
        padded = jnp.concatenate([before, values], axis=0)
        kernels = jnp.concatenate([inner_kernel[layer_at], state_kernel[layer_at]], axis=0)
        pre_act = (
            jnp.zeros_like(values)
            + jnp.concatenate([inner_bias[layer_at], state_bias[layer_at]])[None, :]
        )
        for offset in range(KERNEL):
            same_seq = (seg_early[offset : offset + tok_rows] == segments).astype(jnp.float32)
            pre_act = (
                pre_act
                + kernels[:, offset][None, :]
                * padded[offset : offset + tok_rows]
                * same_seq[:, None]
            )
        post_act = jax.nn.silu(pre_act)
        post_x = post_act[:, :inner_cols]
        b_mat = post_act[:, inner_cols : inner_cols + state_half]
        c_mat = post_act[:, inner_cols + state_half :]
        pieces = mixer_parts(
            post_x,
            b_mat,
            c_mat,
            raw_step,
            step_bias[layer_at],
            decay_log[layer_at],
            skip_gain[layer_at],
            segments,
            seg_prior,
        )
        unused, entry_state = carried_in(
            (pieces[6], pieces[5]),
            "row",
            link_up,
            (jnp.ones_like(pieces[6]), jnp.zeros_like(pieces[5])),
            False,
        )
        mixed_out = mixer_finish(pieces, entry_state)
        silu_gate = jax.nn.silu(gate_val)
        gated = mixed_out * silu_gate
        power_sum = row_total(jnp.sum(gated * gated, axis=1))
        gated_scale = lax.rsqrt(power_sum / inner_full + EPSILON)
        normed_y = (gated * gated_scale[:, None] * gated_gain[layer_at][None, :]).astype(
            jnp.bfloat16
        )
        partial_out = jnp.dot(normed_y, output_full, preferred_element_type=jnp.float32)
        stored = None
        saved.append(
            (
                resid,
                row_scale,
                normed_all,
                gate_val,
                padded,
                pre_act,
                post_x,
                b_mat,
                c_mat,
                raw_step,
                entry_state,
                pieces[4],
                pieces[1],
                pieces[6],
                mixed_out,
                silu_gate,
                gated,
                gated_scale,
                normed_y,
                stored,
            )
        )
        if layer_at + 1 < LAYERS:
            resid, new_scale, normed_all = forward_turn(
                partial_out, resid, norm_gain[layer_at + 1]
            )
            row_scale = new_scale[:, 0]
        else:
            resid = resid + lax.psum_scatter(partial_out, "col", scatter_dimension=1, tiled=True)
    layer_output = resid.astype(jnp.bfloat16)
    resid_grad = cotangent.astype(jnp.float32)
    big_grads = [None] * LAYERS
    small_terms = [None] * LAYERS
    for layer_at in reversed(range(LAYERS)):
        (
            resid,
            row_scale,
            normed_all,
            gate_val,
            padded,
            pre_act,
            post_x,
            b_mat,
            c_mat,
            raw_step,
            entry_state,
            prefix,
            entry_gate,
            dev_decay,
            mixed_out,
            silu_gate,
            gated,
            gated_scale,
            normed_y,
            stored,
        ) = saved[layer_at]
        gate_full, inner_whole, state_full, step_full, output_full = whole_weights[layer_at]
        d_normed_y = lax.dot_general(
            cot_all, output_full, dims_t, preferred_element_type=jnp.float32
        )
        grad_out = lax.dot_general(cot_all, normed_y, dims_w, preferred_element_type=jnp.float32)
        scaled_y = d_normed_y * gated_gain[layer_at][None, :]
        total_y = row_total(jnp.sum(scaled_y * gated, axis=1))
        d_gated = (
            gated_scale[:, None] * scaled_y
            - gated * (gated_scale**3 * total_y / inner_full)[:, None]
        )
        gain_y = jnp.sum(d_normed_y * gated * gated_scale[:, None], axis=0)
        d_mixed = d_gated * silu_gate
        sigma_gate = jax.nn.sigmoid(gate_val)
        d_gate = d_gated * mixed_out * sigma_gate * (1.0 + gate_val * (1.0 - sigma_gate))
        block_count = tok_rows // SPAN
        d_mixed_c = d_mixed.reshape(block_count, SPAN, head_count, -1)
        c_blocks = c_mat.reshape(block_count, SPAN, -1)
        reach_gate = prefix[:, None, :] * entry_gate
        local_pull = jnp.einsum(
            "cih,cihp,cin->hpn", reach_gate, d_mixed_c, c_blocks, precision=HIGHEST
        )
        unused_b, state_pull = carried_in(
            (dev_decay, local_pull),
            "row",
            link_down,
            (jnp.ones_like(dev_decay), jnp.zeros_like(local_pull)),
            True,
        )
        decay_pull = jnp.sum(state_pull * entry_state, axis=(1, 2))

        def local_mixer(px_val, bm_val, cm_val, rs_val, so_val, dr_val, sr_val, es_val):
            return mixer_core(
                px_val, bm_val, cm_val, rs_val, so_val, dr_val, sr_val, es_val, segments, seg_prior
            )

        unused_c, pullback = jax.vjp(
            local_mixer,
            post_x,
            b_mat,
            c_mat,
            raw_step,
            step_bias[layer_at],
            decay_log[layer_at],
            skip_gain[layer_at],
            entry_state,
        )
        d_post_x, grad_b, grad_c, d_raw_step, g_step_bias, g_decay, g_skip, unused_d = pullback(
            (d_mixed, state_pull, decay_pull)
        )
        d_share = lax.psum_scatter(
            jnp.concatenate([grad_b, grad_c], axis=1), "col", scatter_dimension=1, tiled=True
        )
        d_post = jnp.concatenate([d_post_x, d_share], axis=1)
        share_pre = lax.dynamic_slice_in_dim(
            pre_act[:, inner_cols:], col_at * share_cols, share_cols, 1
        )
        own_pre = jnp.concatenate([pre_act[:, :inner_cols], share_pre], axis=1)
        sigma_pre = jax.nn.sigmoid(own_pre)
        d_pre = d_post * sigma_pre * (1.0 + own_pre * (1.0 - sigma_pre))
        after_rows = passed_along(d_pre[: KERNEL - 1], "row", -1)
        d_pre_ext = jnp.concatenate([d_pre, after_rows], axis=0)
        share_kernel = lax.dynamic_slice_in_dim(
            state_kernel[layer_at], col_at * share_cols, share_cols, 0
        )
        own_kernel = jnp.concatenate([inner_kernel[layer_at], share_kernel], axis=0)
        share_padded = lax.dynamic_slice_in_dim(
            padded[:, inner_cols:], col_at * share_cols, share_cols, 1
        )
        own_padded = jnp.concatenate([padded[:, :inner_cols], share_padded], axis=1)
        d_values = jnp.zeros_like(d_pre)
        kernel_terms = []
        for offset in range(KERNEL):
            lead_by = KERNEL - 1 - offset
            same_back = (seg_late[lead_by : lead_by + tok_rows] == segments).astype(jnp.float32)
            d_values = (
                d_values
                + own_kernel[:, offset][None, :]
                * d_pre_ext[lead_by : lead_by + tok_rows]
                * same_back[:, None]
            )
            same_fwd = (seg_early[offset : offset + tok_rows] == segments).astype(jnp.float32)
            kernel_terms.append(
                jnp.sum(d_pre * own_padded[offset : offset + tok_rows] * same_fwd[:, None], axis=0)
            )
        kernel_grad = jnp.stack(kernel_terms, axis=0)
        bias_grad = jnp.sum(d_pre, axis=0)
        d_gate16 = d_gate.astype(jnp.bfloat16)
        d_inner16 = d_values[:, :inner_cols].astype(jnp.bfloat16)
        d_pair16 = d_values[:, inner_cols:].astype(jnp.bfloat16)
        d_step16 = d_raw_step.astype(jnp.bfloat16)
        share_weight = lax.dynamic_slice_in_dim(state_full, col_at * share_cols, share_cols, 1)
        partial_in = lax.dot_general(
            d_gate16, gate_full, dims_t, preferred_element_type=jnp.float32
        )
        partial_in = partial_in + lax.dot_general(
            d_inner16, inner_whole, dims_t, preferred_element_type=jnp.float32
        )
        partial_in = partial_in + lax.dot_general(
            d_pair16, share_weight, dims_t, preferred_element_type=jnp.float32
        )
        partial_in = partial_in + lax.dot_general(
            d_step16, step_full, dims_t, preferred_element_type=jnp.float32
        )
        low_grads = jnp.concatenate([d_gate16, d_inner16, d_pair16, d_step16], axis=1)
        grad_in = lax.dot_general(normed_all, low_grads, dims_w, preferred_element_type=jnp.float32)
        layer_grads = jnp.concatenate(
            [grad_out.astype(jnp.bfloat16), grad_in.astype(jnp.bfloat16)], axis=1
        )
        layer_grads = jnp.pad(layer_grads, ((0, 0), (0, -layer_grads.shape[1] % 128)))
        big_grads[layer_at] = lax.psum_scatter(
            layer_grads, ("dp", "row"), scatter_dimension=0, tiled=True
        ).astype(jnp.float32)
        turned = backward_turn(
            partial_in, resid_grad, resid, row_scale, norm_gain[layer_at], layer_at > 0
        )
        resid_grad, gain_in = turned[0], turned[1][0]
        if layer_at > 0:
            cot_all = turned[2]
        small_terms[layer_at] = (
            gain_in,
            gain_y,
            kernel_grad[:, :inner_cols],
            bias_grad[:inner_cols],
            kernel_grad[:, inner_cols:],
            bias_grad[inner_cols:],
            g_step_bias,
            g_decay,
            g_skip,
        )

    model_cols = output_weight.shape[1]
    sizes = (model_cols, inner_cols, inner_cols, share_cols, head_count)
    summed, at = [], 0
    for size in sizes:
        summed.append(jnp.stack([big[:, at : at + size] for big in big_grads], axis=0))
        at += size
    shapes = [part.shape for terms in small_terms for part in terms]
    unpacked = unpacked_small(
        small_total(packed_small([part for terms in small_terms for part in terms])), shapes
    )
    count = len(small_terms[0])
    smalls = [
        jnp.stack([unpacked[layer_at * count + slot] for layer_at in range(LAYERS)], axis=0)
        for slot in range(count)
    ]
    return (
        layer_output,
        resid_grad,
        smalls[0],
        summed[1],
        summed[2],
        summed[3],
        summed[4],
        jnp.swapaxes(smalls[2], 1, 2),
        smalls[3],
        jnp.swapaxes(smalls[4], 1, 2),
        smalls[5],
        smalls[6],
        smalls[7],
        smalls[8],
        smalls[1],
        jnp.transpose(summed[0], (0, 2, 1)),
    )


def solution(mesh):
    placed = (
        P(("dp", "row"), "col"),
        P("dp", None),
        P(("dp", "row"), "col"),
        P(None, "col"),
        P(None, "row", "col"),
        P(None, "row", "col"),
        P(None, "row", None),
        P(None, "row", "col"),
        P(None, "col", None),
        P(None, "col"),
        P(),
        P(),
        P(None, "col"),
        P(None, "col"),
        P(None, "col"),
        P(None, "col"),
        P(None, "col", "row"),
    )
    return jax.shard_map(
        local,
        mesh=mesh,
        in_specs=placed,
        out_specs=(
            P(("dp", "row"), "col"),
            P(("dp", "row"), "col"),
            P(None, "col"),
            P(None, ("dp", "row"), "col"),
            P(None, ("dp", "row"), "col"),
            P(None, ("dp", "row"), "col"),
            P(None, ("dp", "row"), "col"),
            P(None, "col", None),
            P(None, "col"),
            P(None, "col", None),
            P(None, "col"),
            P(None, "col"),
            P(None, "col"),
            P(None, "col"),
            P(None, "col"),
            P(None, "col", ("dp", "row")),
        ),
        check_vma=False,
    )
```

```python
import functools

import jax
import jax.numpy as jnp
from jax import lax
from jax.experimental import pallas as pl
from jax.experimental.pallas import tpu as pltpu
from jax.sharding import PartitionSpec as P

KERNEL = 4
SPAN = 256
LAYERS = 2


EPSILON = 1e-05
HIGHEST = lax.Precision.HIGHEST


def passed_along(value, axis, by):
    devices = lax.axis_size(axis)
    pairs = [(i, i + by) for i in range(devices) if 0 <= i + by < devices]
    return lax.ppermute(value, axis, pairs)


def carried_in(part, axis, combine, identity, reverse):
    count = lax.axis_size(axis)
    place = lax.axis_index(axis)
    if count == 2:
        moved = lax.ppermute(part[1], axis, [(1, 0)] if reverse else [(0, 1)])
        return (None, moved)
    ahead = count - 1 - place if reverse else place
    gathered = jax.tree.map(lambda a: lax.all_gather(a, axis), part)
    state = jax.tree.map(lambda a, e: jnp.zeros_like(a) + jnp.asarray(e, a.dtype), part, identity)

    def one(turn, state):
        source = count - 1 - turn if reverse else turn
        return combine(
            state, jax.tree.map(lambda a: lax.dynamic_index_in_dim(a, source, 0, False), gathered)
        )

    return lax.fori_loop(0, ahead, one, state)


MESH = pl.DeviceIdType.MESH
VMEM_SPEC = pl.BlockSpec(memory_space=pltpu.VMEM)
ANY_SPEC = pl.BlockSpec(memory_space=pl.ANY)


def greet(peers):
    barrier = pltpu.get_barrier_semaphore()
    for peer in peers:
        pl.semaphore_signal(barrier, inc=1, device_id=peer, device_id_type=MESH)
    pl.semaphore_wait(barrier, len(peers))


def col_peers(n):
    me = lax.axis_index("col")
    return [{"col": lax.rem(me + k, n)} for k in range(1, n)]


def start_to(peers, src_of, dst, send, recv):
    copies = []
    for k, peer in enumerate(peers):
        copy = pltpu.make_async_remote_copy(
            src_ref=src_of(peer),
            dst_ref=dst,
            send_sem=send.at[k],
            recv_sem=recv.at[k],
            device_id=peer,
            device_id_type=MESH,
        )
        copy.start()
        copies.append(copy)
    return copies


def row_sum_kernel(n, value_ref, total_ref, slots, send, recv):
    me = lax.axis_index("col")
    peers = col_peers(n)
    slots[me] = value_ref[...]
    greet(peers)
    copies = start_to(peers, lambda peer: value_ref, slots.at[me], send, recv)
    for copy in copies:
        copy.wait()
    total = slots[0]
    for k in range(1, n):
        total = total + slots[k]
    total_ref[...] = total


def row_total(values):
    n = lax.axis_size("col")
    return pl.pallas_call(
        functools.partial(row_sum_kernel, n),
        out_shape=jax.ShapeDtypeStruct(values.shape, jnp.float32),
        in_specs=[VMEM_SPEC],
        out_specs=VMEM_SPEC,
        scratch_shapes=[
            pltpu.VMEM((n,) + values.shape, jnp.float32),
            pltpu.SemaphoreType.DMA((n - 1,)),
            pltpu.SemaphoreType.DMA((n - 1,)),
        ],
        compiler_params=pltpu.CompilerParams(
            collective_id=0 if values.shape[0] == 1 else 6, has_side_effects=True
        ),
        name="row_total",
    )(values)


def scatter_sum(n, part_ref, outgoing, arrived, send, recv):
    me = lax.axis_index("col")
    peers = col_peers(n)
    width = outgoing.shape[2]
    for k in range(n):
        outgoing[k] = part_ref[:, k * width : (k + 1) * width].astype(outgoing.dtype)
    greet(peers)
    copies = start_to(peers, lambda peer: outgoing.at[peer["col"]], arrived.at[me], send, recv)
    total = part_ref[:, pl.ds(pl.multiple_of(me * width, width), width)]
    for copy in copies:
        copy.wait()
    for peer in peers:
        total = total + arrived[peer["col"]].astype(jnp.float32)
    return total


def share_kernel_sum(n, part_ref, total_ref, arrived, send, recv):
    me = lax.axis_index("col")
    peers = col_peers(n)
    size = total_ref.shape[0]

    def share(at):
        return pl.ds(pl.multiple_of(at * size, size), size)

    greet(peers)
    copies = start_to(
        peers, lambda peer: part_ref.at[share(peer["col"])], arrived.at[me], send, recv
    )
    arrived[me] = part_ref[share(me), :]
    for copy in copies:
        copy.wait()
    total = arrived[0]
    for k in range(1, n):
        total = total + arrived[k]
    total_ref[...] = total


def share_sum(part):
    n = lax.axis_size("col")
    shape = (part.shape[0] // n, part.shape[1])
    return pl.pallas_call(
        functools.partial(share_kernel_sum, n),
        out_shape=jax.ShapeDtypeStruct(shape, jnp.float32),
        in_specs=[VMEM_SPEC],
        out_specs=VMEM_SPEC,
        scratch_shapes=[
            pltpu.VMEM((n,) + shape, jnp.float32),
            pltpu.SemaphoreType.DMA((n - 1,)),
            pltpu.SemaphoreType.DMA((n - 1,)),
        ],
        compiler_params=pltpu.CompilerParams(collective_id=8, has_side_effects=True),
        name="share_sum",
    )(part)


def rows_over_col(n, product, row_own, row_slots, send, recv):
    me = lax.axis_index("col")
    peers = col_peers(n)
    ones = jnp.ones((8, product.shape[1]), jnp.float32)
    sums = lax.dot_general(
        ones, product, (((1,), (1,)), ((), ())), precision=HIGHEST,
        preferred_element_type=jnp.float32,
    )
    row_own[...] = sums
    row_slots[me] = sums
    copies = start_to(peers, lambda peer: row_own, row_slots.at[me], send, recv)
    for copy in copies:
        copy.wait()
    total = row_slots[0]
    for k in range(1, n):
        total = total + row_slots[k]
    return jnp.transpose(total)[:, :1]


def gather_cols(n, own, all_ref, send, recv):
    me = lax.axis_index("col")
    peers = col_peers(n)
    width = own.shape[1]
    place = all_ref.at[:, pl.ds(pl.multiple_of(me * width, width), width)]
    place[...] = own[...]
    copies = start_to(peers, lambda peer: own, place, send, recv)
    for copy in copies:
        copy.wait()


def forward_turn_kernel(
    n, part_ref, resid_ref, gain_ref, resid_out, scale_out, normed_out,
    outgoing, arrived, row_own, row_slots, own, *sems,
):
    resid = resid_ref[...] + scatter_sum(n, part_ref, outgoing, arrived, sems[0], sems[1])
    resid_out[...] = resid
    square = rows_over_col(n, resid * resid, row_own, row_slots, sems[2], sems[3])
    scale = lax.rsqrt(square / (n * resid.shape[1]) + EPSILON)
    scale_out[...] = scale
    own[...] = (resid * scale * gain_ref[...]).astype(jnp.bfloat16)
    gather_cols(n, own, normed_out, sems[4], sems[5])


def backward_turn_kernel(
    n, spread, part_ref, grad_ref, resid_ref, scale_ref, gain_ref, grad_out, gain_out, *rest
):
    if spread:
        cot_out, rest = rest[0], rest[1:]
    outgoing, arrived, row_own, row_slots, own = rest[:5]
    sems = rest[5:]
    d_normed = scatter_sum(n, part_ref, outgoing, arrived, sems[0], sems[1])
    resid = resid_ref[...]
    scale = scale_ref[...]
    scaled_in = d_normed * gain_ref[...]
    gain_out[...] = jnp.sum(d_normed * resid * scale, axis=0, keepdims=True)
    total = rows_over_col(n, scaled_in * resid, row_own, row_slots, sems[2], sems[3])
    grad = (
        grad_ref[...]
        + scale * scaled_in
        - resid * (scale * scale * scale * total / (n * resid.shape[1]))
    )
    grad_out[...] = grad
    if spread:
        own[...] = grad.astype(jnp.bfloat16)
        gather_cols(n, own, cot_out, sems[4], sems[5])


def turn_scratch(n, rows, width):
    return [
        pltpu.VMEM((n, rows, width), jnp.bfloat16),
        pltpu.VMEM((n, rows, width), jnp.bfloat16),
        pltpu.VMEM((8, rows), jnp.float32),
        pltpu.VMEM((n, 8, rows), jnp.float32),
        pltpu.VMEM((rows, width), jnp.bfloat16),
    ] + [pltpu.SemaphoreType.DMA((n - 1,)) for _ in range(6)]


def forward_turn(part, resid, gain):
    n = lax.axis_size("col")
    rows, width = resid.shape
    return pl.pallas_call(
        functools.partial(forward_turn_kernel, n),
        out_shape=[
            jax.ShapeDtypeStruct((rows, width), jnp.float32),
            jax.ShapeDtypeStruct((rows, 1), jnp.float32),
            jax.ShapeDtypeStruct((rows, n * width), jnp.bfloat16),
        ],
        in_specs=[VMEM_SPEC] * 3,
        out_specs=[VMEM_SPEC] * 3,
        scratch_shapes=turn_scratch(n, rows, width),
        compiler_params=pltpu.CompilerParams(collective_id=1, has_side_effects=True),
        name="forward_turn",
    )(part, resid, gain[None, :])


def backward_turn(part, grad, resid, scale, gain, spread):
    n = lax.axis_size("col")
    rows, width = resid.shape
    outs = [
        jax.ShapeDtypeStruct((rows, width), jnp.float32),
        jax.ShapeDtypeStruct((1, width), jnp.float32),
    ]
    if spread:
        outs.append(jax.ShapeDtypeStruct((rows, n * width), jnp.bfloat16))
    return pl.pallas_call(
        functools.partial(backward_turn_kernel, n, spread),
        out_shape=outs,
        in_specs=[VMEM_SPEC] * 5,
        out_specs=[VMEM_SPEC] * len(outs),
        scratch_shapes=turn_scratch(n, rows, width),
        compiler_params=pltpu.CompilerParams(
            collective_id=2 if spread else 3, has_side_effects=True
        ),
        name="backward_turn" if spread else "backward_end",
    )(part, grad, resid, scale[:, None], gain[None, :])


def entry_kernel(n, tok_ref, gain_ref, tok_all, gain_all, *sems):
    me = lax.axis_index("col")
    peers = col_peers(n)
    width = tok_ref.shape[1]
    place = tok_all.at[:, pl.ds(pl.multiple_of(me * width, width), width)]
    place[...] = tok_ref[...]
    gain_all[me] = gain_ref[...]
    greet(peers)
    copies = start_to(peers, lambda peer: tok_ref, place, sems[0], sems[1])
    copies += start_to(peers, lambda peer: gain_ref, gain_all.at[me], sems[2], sems[3])
    for copy in copies:
        copy.wait()


def entry_gather(tokens, gain):
    n = lax.axis_size("col")
    rows, width = tokens.shape
    return pl.pallas_call(
        functools.partial(entry_kernel, n),
        out_shape=[
            jax.ShapeDtypeStruct((rows, n * width), tokens.dtype),
            jax.ShapeDtypeStruct((n, 1, width), gain.dtype),
        ],
        in_specs=[VMEM_SPEC] * 2,
        out_specs=[VMEM_SPEC] * 2,
        scratch_shapes=[pltpu.SemaphoreType.DMA((n - 1,)) for _ in range(4)],
        compiler_params=pltpu.CompilerParams(collective_id=4, has_side_effects=True),
        name="entry_gather",
    )(tokens, gain[None, :])


def start_pair(src, dst, sems, at, peer):
    copy = pltpu.make_async_remote_copy(
        src_ref=src,
        dst_ref=dst,
        send_sem=sems[0].at[at],
        recv_sem=sems[1].at[at],
        device_id=peer,
        device_id_type=MESH,
    )
    copy.start()
    return copy


def load_kernel(n, axes, tok_ref, cot_ref, gain_ref, *rest):
    count = len(axes)
    weights, rest = rest[:count], rest[count:]
    tok_all, cot_all, gain_all = rest[:3]
    wholes, rest = rest[3 : 3 + count * LAYERS], rest[3 + count * LAYERS :]
    col_sems, across, beside, here = rest[:6], rest[6:8], rest[8:10], rest[10]
    me, at_row, at_dp = lax.axis_index("col"), lax.axis_index("row"), lax.axis_index("dp")
    core = lax.rem(at_dp, 2)
    peers = col_peers(n)
    over = {"row": 1 - at_row}
    twin = {"dp": at_dp + 1 - 2 * core}
    width = tok_ref.shape[1]
    columns = pl.ds(pl.multiple_of(me * width, width), width)
    tok_place, cot_place = tok_all.at[:, columns], cot_all.at[:, columns]
    tok_place[...] = tok_ref[...]
    cot_place[...] = cot_ref[...]
    gain_all[me] = gain_ref[...]
    greet(peers + [over, twin])

    def part(ref, axis, start, size):
        window = pl.ds(pl.multiple_of(start, size), size)
        return ref.at[window] if axis == 0 else ref.at[:, window]

    copies = start_to(peers, lambda peer: tok_ref, tok_place, col_sems[0], col_sems[1])
    copies += start_to(peers, lambda peer: gain_ref, gain_all.at[me], col_sems[2], col_sems[3])
    jobs = []
    for layer_at in range(LAYERS):
        for slot, axis in enumerate(axes):
            at = layer_at * count + slot
            block, whole = weights[slot].at[layer_at], wholes[at]
            size = block.shape[axis]
            half = size // 2
            sent = start_pair(
                part(block, axis, core * half, half),
                part(whole, axis, at_row * size + core * half, half),
                across,
                at,
                over,
            )
            kept = pltpu.make_async_copy(
                block, part(whole, axis, at_row * size, size), here.at[at]
            )
            kept.start()
            jobs.append((sent, kept, whole, axis, size, half))
    copies += start_to(peers, lambda peer: cot_ref, cot_place, col_sems[4], col_sems[5])
    passed = []
    for at, (sent, kept, whole, axis, size, half) in enumerate(jobs):
        sent.wait_recv()
        landed = part(whole, axis, (1 - at_row) * size + core * half, half)
        passed.append(start_pair(landed, landed, beside, at, twin))
    for sent, kept, *unused in jobs:
        sent.wait_send()
        kept.wait()
    for copy in passed + copies:
        copy.wait()


def load_all(tokens, cotangent, gain, weights, axes):
    n = lax.axis_size("col")
    rows, width = tokens.shape
    outs = [
        jax.ShapeDtypeStruct((rows, n * width), tokens.dtype),
        jax.ShapeDtypeStruct((rows, n * width), cotangent.dtype),
        jax.ShapeDtypeStruct((n, 1, width), gain.dtype),
    ]
    for layer_at in range(LAYERS):
        for weight, axis in zip(weights, axes):
            shape = list(weight.shape[1:])
            shape[axis] *= 2
            outs.append(jax.ShapeDtypeStruct(tuple(shape), weight.dtype))
    count = len(weights) * LAYERS
    return pl.pallas_call(
        functools.partial(load_kernel, n, axes),
        out_shape=outs,
        in_specs=[VMEM_SPEC] * 3 + [ANY_SPEC] * len(weights),
        out_specs=[VMEM_SPEC] * 3 + [ANY_SPEC] * count,
        scratch_shapes=[pltpu.SemaphoreType.DMA((n - 1,)) for _ in range(6)]
        + [pltpu.SemaphoreType.DMA((count,)) for _ in range(5)],
        compiler_params=pltpu.CompilerParams(collective_id=7, has_side_effects=True),
        name="load_all",
    )(tokens, cotangent, gain[None, :], *weights)


def small_kernel(dp, row, value_ref, total_ref, slots, send, recv):
    at_dp, at_row = lax.axis_index("dp"), lax.axis_index("row")
    me = at_dp * row + at_row
    peers = []
    for k in range(1, dp * row):
        peers.append(
            {"dp": lax.rem(at_dp + k // row, dp), "row": lax.rem(at_row + k % row, row)}
        )
    slots[me] = value_ref[...]
    greet(peers)
    copies = start_to(peers, lambda peer: value_ref, slots.at[me], send, recv)
    for copy in copies:
        copy.wait()
    total = slots[0]
    for k in range(1, dp * row):
        total = total + slots[k]
    total_ref[...] = total


def small_total(value):
    dp, row = lax.axis_size("dp"), lax.axis_size("row")
    count = dp * row
    if count > 8:
        return lax.psum(value, ("dp", "row"))
    return pl.pallas_call(
        functools.partial(small_kernel, dp, row),
        out_shape=jax.ShapeDtypeStruct(value.shape, jnp.float32),
        in_specs=[VMEM_SPEC],
        out_specs=VMEM_SPEC,
        scratch_shapes=[
            pltpu.VMEM((count,) + value.shape, jnp.float32),
            pltpu.SemaphoreType.DMA((count - 1,)),
            pltpu.SemaphoreType.DMA((count - 1,)),
        ],
        compiler_params=pltpu.CompilerParams(collective_id=5, has_side_effects=True),
        name="small_total",
    )(value)


def whole_over_row(block, axis):
    if lax.axis_size("row") != 2:
        return lax.all_gather(block, "row", axis=axis, tiled=True)
    other = lax.ppermute(block, "row", [(0, 1), (1, 0)])
    size = block.shape[axis]
    trio = jnp.concatenate([block, other, block], axis=axis)
    return lax.dynamic_slice_in_dim(trio, lax.axis_index("row") * size, 2 * size, axis)


def whole_over_col(block):
    n = lax.axis_size("col")
    size = block.shape[1]
    blocks = [block]
    for k in range(1, n):
        blocks.append(lax.ppermute(block, "col", [(i, (i - k) % n) for i in range(n)]))
    twice = jnp.concatenate(blocks + blocks[:-1], axis=1)
    start = lax.rem(n - lax.axis_index("col"), n) * size
    return lax.dynamic_slice_in_dim(twice, start, n * size, 1)


def packed_small(parts):
    flat = jnp.concatenate([part.reshape(-1) for part in parts])
    total = flat.shape[0]
    lines = -(-total // 1024) * 8
    return jnp.pad(flat, (0, lines * 128 - total)).reshape(lines, 128)


def unpacked_small(packed, shapes):
    flat = packed.reshape(-1)
    out, at = [], 0
    for shape in shapes:
        size = 1
        for extent in shape:
            size *= extent
        out.append(flat[at : at + size].reshape(shape))
        at += size
    return out


def link_up(earlier, later):
    return (earlier[0] * later[0], later[0][:, None, None] * earlier[1] + later[1])


def link_down(earlier, later):
    return (earlier[0] * later[0], later[1] + later[0][:, None, None] * earlier[1])


def mixer_parts(
    post_x, b_mat, c_mat, raw_step, step_off, decay_rate, skip_rate, segments, seg_prior
):
    tok_count = post_x.shape[0]
    head_count = raw_step.shape[1]
    head_width = post_x.shape[1] // head_count
    block_count = tok_count // SPAN
    step_size = jax.nn.softplus(raw_step + step_off[None, :])
    decay_now = -jnp.exp(decay_rate)[None, :] * step_size
    xs_c = post_x.reshape(block_count, SPAN, head_count, head_width)
    step_c = step_size.reshape(block_count, SPAN, head_count)
    cumulative = jnp.cumsum(decay_now.reshape(block_count, SPAN, head_count), axis=1)
    b_c = b_mat.reshape(block_count, SPAN, -1)
    c_c = c_mat.reshape(block_count, SPAN, -1)
    seg_c = segments.reshape(block_count, SPAN)
    places = jnp.arange(SPAN)
    same_seq = (seg_c[:, :, None] == seg_c[:, None, :]) & (places[:, None] >= places[None, :])[None]
    causal = same_seq.astype(jnp.float32)[:, None, :, :]
    cum_heads = jnp.transpose(cumulative, (0, 2, 1))
    step_heads = jnp.transpose(step_c, (0, 2, 1))
    spread = cum_heads[:, :, :, None] - cum_heads[:, :, None, :]
    scores = jnp.einsum("cin,cjn->cij", c_c, b_c, precision=HIGHEST)
    weights = jnp.exp(spread * causal) * causal * scores[:, None, :, :] * step_heads[:, :, None, :]
    intra_part = jnp.einsum("chij,cjhp->cihp", weights, xs_c, precision=HIGHEST)
    entry_gate = jnp.exp(cumulative) * (seg_c == seg_prior[:, None]).astype(jnp.float32)[..., None]
    tail_gate = (
        jnp.exp(cumulative[:, -1:, :] - cumulative)
        * (seg_c == seg_c[:, -1:]).astype(jnp.float32)[..., None]
        * step_c
    )
    fresh_state = jnp.einsum("cjh,cjhp,cjn->chpn", tail_gate, xs_c, b_c, precision=HIGHEST)
    block_decay = (
        jnp.exp(cumulative[:, -1, :]) * (seg_c[:, -1] == seg_prior).astype(jnp.float32)[:, None]
    )

    def advance(state_now, element):
        return (element[1][:, None, None] * state_now + element[0], state_now)

    dev_state, starts = lax.scan(
        advance, jnp.zeros_like(fresh_state[0]), (fresh_state, block_decay)
    )
    prefix = jnp.cumprod(
        jnp.concatenate([jnp.ones_like(block_decay), block_decay[:-1]], axis=0), axis=0
    )
    dev_decay = prefix[-1] * block_decay[-1]
    local_part = intra_part + skip_rate[None, None, :, None] * xs_c
    return (local_part, entry_gate, c_c, starts, prefix, dev_state, dev_decay)


def mixer_finish(pieces, entry_state):
    local_part, entry_gate, c_c, starts, prefix, dev_state, dev_decay = pieces
    states = starts + prefix[:, :, None, None] * entry_state[None]
    incoming = jnp.einsum("chpn,cin->cihp", states, c_c, precision=HIGHEST)
    mixed_out = local_part + entry_gate[..., None] * incoming
    return mixed_out.reshape(mixed_out.shape[0] * SPAN, -1)


def mixer_core(
    post_x,
    b_mat,
    c_mat,
    raw_step,
    step_off,
    decay_rate,
    skip_rate,
    entry_state,
    segments,
    seg_prior,
):
    pieces = mixer_parts(
        post_x, b_mat, c_mat, raw_step, step_off, decay_rate, skip_rate, segments, seg_prior
    )
    return (mixer_finish(pieces, entry_state), pieces[5], pieces[6])


def local(
    tokens,
    segment_index,
    cotangent,
    norm_gain,
    gate_weight,
    inner_weight,
    state_weight,
    step_weight,
    inner_kernel,
    inner_bias,
    state_kernel,
    state_bias,
    step_bias,
    decay_log,
    skip_gain,
    gated_gain,
    output_weight,
):
    tok_rows = tokens.shape[0]
    full_width = tokens.shape[1] * lax.axis_size("col")
    head_count = step_bias.shape[1]
    inner_cols = inner_kernel.shape[1]
    inner_full = inner_cols * lax.axis_size("col")
    state_cols = state_kernel.shape[1]
    state_half = state_cols // 2
    share_cols = state_cols // lax.axis_size("col")
    col_at = lax.axis_index("col")
    first_tok = lax.axis_index("row") * tok_rows
    group_seg = segment_index[0]
    seg_front = jnp.concatenate([jnp.full((KERNEL - 1,), -1, jnp.int32), group_seg])
    seg_rear = jnp.concatenate([group_seg, jnp.full((KERNEL - 1,), -2, jnp.int32)])
    seg_early = lax.dynamic_slice_in_dim(seg_front, first_tok, tok_rows + KERNEL - 1)
    seg_late = lax.dynamic_slice_in_dim(seg_rear, first_tok, tok_rows + KERNEL - 1)
    segments = seg_early[KERNEL - 1 :]
    seg_prior = jnp.concatenate(
        [seg_early[KERNEL - 2 : KERNEL - 1], segments[SPAN - 1 : -1 : SPAN]]
    )
    dims_t = (((1,), (1,)), ((), ()))
    dims_w = (((0,), (0,)), ((), ()))
    resid = tokens.astype(jnp.float32)
    paired = lax.axis_size("row") == 2 and lax.axis_size("dp") % 2 == 0
    if paired:
        tokens_all, cot_all, gain_all, *wholes = load_all(
            tokens,
            cotangent,
            norm_gain[0],
            (gate_weight, inner_weight, state_weight, output_weight),
            (0, 0, 0, 1),
        )
    else:
        tokens_all, gain_all = entry_gather(tokens, norm_gain[0])
        cot_all = whole_over_col(cotangent)
    first_all = tokens_all.astype(jnp.float32)
    row_scale = lax.rsqrt(jnp.sum(first_all * first_all, axis=1) / full_width + EPSILON)
    normed_all = (first_all * row_scale[:, None] * gain_all.reshape(1, -1)).astype(jnp.bfloat16)
    whole_weights = []
    for layer_at in range(LAYERS):
        step_full = whole_over_row(step_weight[layer_at], 0)
        if paired:
            gate_full, inner_whole, state_full, output_full = wholes[
                4 * layer_at : 4 * layer_at + 4
            ]
        else:
            gate_full = whole_over_row(gate_weight[layer_at], 0)
            inner_whole = whole_over_row(inner_weight[layer_at], 0)
            state_full = whole_over_row(state_weight[layer_at], 0)
            output_full = whole_over_row(output_weight[layer_at], 1)
        whole_weights.append((gate_full, inner_whole, state_full, step_full, output_full))
    saved = []
    for layer_at in range(LAYERS):
        gate_full, inner_whole, state_full, step_full, output_full = whole_weights[layer_at]
        gate_val = jnp.dot(normed_all, gate_full, preferred_element_type=jnp.float32)
        inner_val = jnp.dot(normed_all, inner_whole, preferred_element_type=jnp.float32)
        pair_val = jnp.dot(normed_all, state_full, preferred_element_type=jnp.float32)
        raw_step = jnp.dot(normed_all, step_full, preferred_element_type=jnp.float32)
        values = jnp.concatenate([inner_val, pair_val], axis=1)
        before = passed_along(values[tok_rows - (KERNEL - 1) :], "row", 1)
        padded = jnp.concatenate([before, values], axis=0)
        kernels = jnp.concatenate([inner_kernel[layer_at], state_kernel[layer_at]], axis=0)
        pre_act = (
            jnp.zeros_like(values)
            + jnp.concatenate([inner_bias[layer_at], state_bias[layer_at]])[None, :]
        )
        for offset in range(KERNEL):
            same_seq = (seg_early[offset : offset + tok_rows] == segments).astype(jnp.float32)
            pre_act = (
                pre_act
                + kernels[:, offset][None, :]
                * padded[offset : offset + tok_rows]
                * same_seq[:, None]
            )
        post_act = jax.nn.silu(pre_act)
        post_x = post_act[:, :inner_cols]
        b_mat = post_act[:, inner_cols : inner_cols + state_half]
        c_mat = post_act[:, inner_cols + state_half :]
        pieces = mixer_parts(
            post_x,
            b_mat,
            c_mat,
            raw_step,
            step_bias[layer_at],
            decay_log[layer_at],
            skip_gain[layer_at],
            segments,
            seg_prior,
        )
        unused, entry_state = carried_in(
            (pieces[6], pieces[5]),
            "row",
            link_up,
            (jnp.ones_like(pieces[6]), jnp.zeros_like(pieces[5])),
            False,
        )
        mixed_out = mixer_finish(pieces, entry_state)
        silu_gate = jax.nn.silu(gate_val)
        gated = mixed_out * silu_gate
        power_part = jnp.sum(gated * gated, axis=1)
        if layer_at + 1 < LAYERS:
            power_sum = row_total(power_part[None, :])[0]
        else:
            last_dyn = lax.dot_general(
                cot_all, output_full, dims_t, preferred_element_type=jnp.float32
            )
            last_scaled = last_dyn * gated_gain[layer_at][None, :]
            power_sum, last_total = row_total(
                jnp.stack([power_part, jnp.sum(last_scaled * gated, axis=1)], axis=0)
            )
        gated_scale = lax.rsqrt(power_sum / inner_full + EPSILON)
        normed_y = (gated * gated_scale[:, None] * gated_gain[layer_at][None, :]).astype(
            jnp.bfloat16
        )
        partial_out = jnp.dot(normed_y, output_full, preferred_element_type=jnp.float32)
        stored = None
        saved.append(
            (
                resid,
                row_scale,
                normed_all,
                gate_val,
                padded,
                pre_act,
                post_x,
                b_mat,
                c_mat,
                raw_step,
                entry_state,
                pieces[4],
                pieces[1],
                pieces[6],
                mixed_out,
                silu_gate,
                gated,
                gated_scale,
                normed_y,
                stored,
            )
        )
        if layer_at + 1 < LAYERS:
            resid, new_scale, normed_all = forward_turn(
                partial_out, resid, norm_gain[layer_at + 1]
            )
            row_scale = new_scale[:, 0]
        else:
            resid = resid + lax.psum_scatter(partial_out, "col", scatter_dimension=1, tiled=True)
    layer_output = resid.astype(jnp.bfloat16)
    resid_grad = cotangent.astype(jnp.float32)
    big_grads = [None] * LAYERS
    small_terms = [None] * LAYERS
    for layer_at in reversed(range(LAYERS)):
        (
            resid,
            row_scale,
            normed_all,
            gate_val,
            padded,
            pre_act,
            post_x,
            b_mat,
            c_mat,
            raw_step,
            entry_state,
            prefix,
            entry_gate,
            dev_decay,
            mixed_out,
            silu_gate,
            gated,
            gated_scale,
            normed_y,
            stored,
        ) = saved[layer_at]
        gate_full, inner_whole, state_full, step_full, output_full = whole_weights[layer_at]
        if layer_at + 1 < LAYERS:
            d_normed_y = lax.dot_general(
                cot_all, output_full, dims_t, preferred_element_type=jnp.float32
            )
        else:
            d_normed_y = last_dyn
        grad_out = lax.dot_general(cot_all, normed_y, dims_w, preferred_element_type=jnp.float32)
        scaled_y = d_normed_y * gated_gain[layer_at][None, :]
        if layer_at + 1 < LAYERS:
            total_y = row_total(jnp.sum(scaled_y * gated, axis=1)[None, :])[0]
        else:
            total_y = last_total
        d_gated = (
            gated_scale[:, None] * scaled_y
            - gated * (gated_scale**3 * total_y / inner_full)[:, None]
        )
        gain_y = jnp.sum(d_normed_y * gated * gated_scale[:, None], axis=0)
        d_mixed = d_gated * silu_gate
        sigma_gate = jax.nn.sigmoid(gate_val)
        d_gate = d_gated * mixed_out * sigma_gate * (1.0 + gate_val * (1.0 - sigma_gate))
        block_count = tok_rows // SPAN
        d_mixed_c = d_mixed.reshape(block_count, SPAN, head_count, -1)
        c_blocks = c_mat.reshape(block_count, SPAN, -1)
        reach_gate = prefix[:, None, :] * entry_gate
        local_pull = jnp.einsum(
            "cih,cihp,cin->hpn", reach_gate, d_mixed_c, c_blocks, precision=HIGHEST
        )
        unused_b, state_pull = carried_in(
            (dev_decay, local_pull),
            "row",
            link_down,
            (jnp.ones_like(dev_decay), jnp.zeros_like(local_pull)),
            True,
        )
        decay_pull = jnp.sum(state_pull * entry_state, axis=(1, 2))

        def local_mixer(px_val, bm_val, cm_val, rs_val, so_val, dr_val, sr_val, es_val):
            return mixer_core(
                px_val, bm_val, cm_val, rs_val, so_val, dr_val, sr_val, es_val, segments, seg_prior
            )

        unused_c, pullback = jax.vjp(
            local_mixer,
            post_x,
            b_mat,
            c_mat,
            raw_step,
            step_bias[layer_at],
            decay_log[layer_at],
            skip_gain[layer_at],
            entry_state,
        )
        d_post_x, grad_b, grad_c, d_raw_step, g_step_bias, g_decay, g_skip, unused_d = pullback(
            (d_mixed, state_pull, decay_pull)
        )
        d_share = share_sum(jnp.concatenate([grad_b.T, grad_c.T], axis=0)).T
        d_post = jnp.concatenate([d_post_x, d_share], axis=1)
        share_pre = lax.dynamic_slice_in_dim(
            pre_act[:, inner_cols:], col_at * share_cols, share_cols, 1
        )
        own_pre = jnp.concatenate([pre_act[:, :inner_cols], share_pre], axis=1)
        sigma_pre = jax.nn.sigmoid(own_pre)
        d_pre = d_post * sigma_pre * (1.0 + own_pre * (1.0 - sigma_pre))
        after_rows = passed_along(d_pre[: KERNEL - 1], "row", -1)
        d_pre_ext = jnp.concatenate([d_pre, after_rows], axis=0)
        share_kernel = lax.dynamic_slice_in_dim(
            state_kernel[layer_at], col_at * share_cols, share_cols, 0
        )
        own_kernel = jnp.concatenate([inner_kernel[layer_at], share_kernel], axis=0)
        share_padded = lax.dynamic_slice_in_dim(
            padded[:, inner_cols:], col_at * share_cols, share_cols, 1
        )
        own_padded = jnp.concatenate([padded[:, :inner_cols], share_padded], axis=1)
        d_values = jnp.zeros_like(d_pre)
        kernel_terms = []
        for offset in range(KERNEL):
            lead_by = KERNEL - 1 - offset
            same_back = (seg_late[lead_by : lead_by + tok_rows] == segments).astype(jnp.float32)
            d_values = (
                d_values
                + own_kernel[:, offset][None, :]
                * d_pre_ext[lead_by : lead_by + tok_rows]
                * same_back[:, None]
            )
            same_fwd = (seg_early[offset : offset + tok_rows] == segments).astype(jnp.float32)
            kernel_terms.append(
                jnp.sum(d_pre * own_padded[offset : offset + tok_rows] * same_fwd[:, None], axis=0)
            )
        kernel_grad = jnp.stack(kernel_terms, axis=0)
        bias_grad = jnp.sum(d_pre, axis=0)
        d_gate16 = d_gate.astype(jnp.bfloat16)
        d_inner16 = d_values[:, :inner_cols].astype(jnp.bfloat16)
        d_pair16 = d_values[:, inner_cols:].astype(jnp.bfloat16)
        d_step16 = d_raw_step.astype(jnp.bfloat16)
        share_weight = lax.dynamic_slice_in_dim(state_full, col_at * share_cols, share_cols, 1)
        partial_in = lax.dot_general(
            d_gate16, gate_full, dims_t, preferred_element_type=jnp.float32
        )
        partial_in = partial_in + lax.dot_general(
            d_inner16, inner_whole, dims_t, preferred_element_type=jnp.float32
        )
        partial_in = partial_in + lax.dot_general(
            d_pair16, share_weight, dims_t, preferred_element_type=jnp.float32
        )
        partial_in = partial_in + lax.dot_general(
            d_step16, step_full, dims_t, preferred_element_type=jnp.float32
        )
        low_grads = jnp.concatenate([d_gate16, d_inner16, d_pair16, d_step16], axis=1)
        low_grads = jnp.pad(low_grads, ((0, 0), (0, -low_grads.shape[1] % 128)))
        grad_in = lax.dot_general(normed_all, low_grads, dims_w, preferred_element_type=jnp.float32)
        layer_grads = jnp.concatenate(
            [grad_out.astype(jnp.bfloat16), grad_in.astype(jnp.bfloat16)], axis=1
        )
        if layer_at > 0:
            layer_grads, partial_in = lax.optimization_barrier((layer_grads, partial_in))
        big_grads[layer_at] = lax.psum_scatter(
            layer_grads, ("dp", "row"), scatter_dimension=0, tiled=True
        ).astype(jnp.float32)
        turned = backward_turn(
            partial_in, resid_grad, resid, row_scale, norm_gain[layer_at], layer_at > 0
        )
        resid_grad, gain_in = turned[0], turned[1][0]
        if layer_at > 0:
            cot_all = turned[2]
        small_terms[layer_at] = (
            gain_in,
            gain_y,
            kernel_grad[:, :inner_cols],
            bias_grad[:inner_cols],
            kernel_grad[:, inner_cols:],
            bias_grad[inner_cols:],
            g_step_bias,
            g_decay,
            g_skip,
        )

    model_cols = output_weight.shape[1]
    sizes = (model_cols, inner_cols, inner_cols, share_cols, head_count)
    summed, at = [], 0
    for size in sizes:
        summed.append(jnp.stack([big[:, at : at + size] for big in big_grads], axis=0))
        at += size
    shapes = [part.shape for terms in small_terms for part in terms]
    unpacked = unpacked_small(
        small_total(packed_small([part for terms in small_terms for part in terms])), shapes
    )
    count = len(small_terms[0])
    smalls = [
        jnp.stack([unpacked[layer_at * count + slot] for layer_at in range(LAYERS)], axis=0)
        for slot in range(count)
    ]
    return (
        layer_output,
        resid_grad,
        smalls[0],
        summed[1],
        summed[2],
        summed[3],
        summed[4],
        jnp.swapaxes(smalls[2], 1, 2),
        smalls[3],
        jnp.swapaxes(smalls[4], 1, 2),
        smalls[5],
        smalls[6],
        smalls[7],
        smalls[8],
        smalls[1],
        jnp.transpose(summed[0], (0, 2, 1)),
    )


def solution(mesh):
    placed = (
        P(("dp", "row"), "col"),
        P("dp", None),
        P(("dp", "row"), "col"),
        P(None, "col"),
        P(None, "row", "col"),
        P(None, "row", "col"),
        P(None, "row", None),
        P(None, "row", "col"),
        P(None, "col", None),
        P(None, "col"),
        P(),
        P(),
        P(None, "col"),
        P(None, "col"),
        P(None, "col"),
        P(None, "col"),
        P(None, "col", "row"),
    )
    return jax.shard_map(
        local,
        mesh=mesh,
        in_specs=placed,
        out_specs=(
            P(("dp", "row"), "col"),
            P(("dp", "row"), "col"),
            P(None, "col"),
            P(None, ("dp", "row"), "col"),
            P(None, ("dp", "row"), "col"),
            P(None, ("dp", "row"), "col"),
            P(None, ("dp", "row"), "col"),
            P(None, "col", None),
            P(None, "col"),
            P(None, "col", None),
            P(None, "col"),
            P(None, "col"),
            P(None, "col"),
            P(None, "col"),
            P(None, "col"),
            P(None, "col", ("dp", "row")),
        ),
        check_vma=False,
    )
```

```python
import functools

import jax
import jax.numpy as jnp
from jax import lax
from jax.experimental import pallas as pl
from jax.experimental.pallas import tpu as pltpu
from jax.sharding import PartitionSpec as P

KERNEL = 4
SPAN = 256
LAYERS = 2


EPSILON = 1e-05
HIGHEST = lax.Precision.HIGHEST


def passed_along(value, axis, by):
    devices = lax.axis_size(axis)
    pairs = [(i, i + by) for i in range(devices) if 0 <= i + by < devices]
    return lax.ppermute(value, axis, pairs)


def carried_in(part, axis, combine, identity, reverse):
    count = lax.axis_size(axis)
    place = lax.axis_index(axis)
    if count == 2:
        moved = lax.ppermute(part[1], axis, [(1, 0)] if reverse else [(0, 1)])
        return (None, moved)
    ahead = count - 1 - place if reverse else place
    gathered = jax.tree.map(lambda a: lax.all_gather(a, axis), part)
    state = jax.tree.map(lambda a, e: jnp.zeros_like(a) + jnp.asarray(e, a.dtype), part, identity)

    def one(turn, state):
        source = count - 1 - turn if reverse else turn
        return combine(
            state, jax.tree.map(lambda a: lax.dynamic_index_in_dim(a, source, 0, False), gathered)
        )

    return lax.fori_loop(0, ahead, one, state)


MESH = pl.DeviceIdType.MESH
VMEM_SPEC = pl.BlockSpec(memory_space=pltpu.VMEM)


def greet(peers):
    barrier = pltpu.get_barrier_semaphore()
    for peer in peers:
        pl.semaphore_signal(barrier, inc=1, device_id=peer, device_id_type=MESH)
    pl.semaphore_wait(barrier, len(peers))


def col_peers(n):
    me = lax.axis_index("col")
    return [{"col": lax.rem(me + k, n)} for k in range(1, n)]


def start_to(peers, src_of, dst, send, recv):
    copies = []
    for k, peer in enumerate(peers):
        copy = pltpu.make_async_remote_copy(
            src_ref=src_of(peer),
            dst_ref=dst,
            send_sem=send.at[k],
            recv_sem=recv.at[k],
            device_id=peer,
            device_id_type=MESH,
        )
        copy.start()
        copies.append(copy)
    return copies


def row_sum_kernel(n, value_ref, total_ref, slots, send, recv):
    me = lax.axis_index("col")
    peers = col_peers(n)
    slots[me] = value_ref[...]
    greet(peers)
    copies = start_to(peers, lambda peer: value_ref, slots.at[me], send, recv)
    for copy in copies:
        copy.wait()
    total = slots[0]
    for k in range(1, n):
        total = total + slots[k]
    total_ref[...] = total


def row_total(values):
    n = lax.axis_size("col")
    return pl.pallas_call(
        functools.partial(row_sum_kernel, n),
        out_shape=jax.ShapeDtypeStruct(values.shape, jnp.float32),
        in_specs=[VMEM_SPEC],
        out_specs=VMEM_SPEC,
        scratch_shapes=[
            pltpu.VMEM((n,) + values.shape, jnp.float32),
            pltpu.SemaphoreType.DMA((n - 1,)),
            pltpu.SemaphoreType.DMA((n - 1,)),
        ],
        compiler_params=pltpu.CompilerParams(
            collective_id=0 if values.shape[0] == 1 else 6, has_side_effects=True
        ),
        name="row_total",
    )(values)


def scatter_sum(n, part_ref, outgoing, arrived, send, recv):
    me = lax.axis_index("col")
    peers = col_peers(n)
    width = outgoing.shape[2]
    for k in range(n):
        outgoing[k] = part_ref[:, k * width : (k + 1) * width].astype(outgoing.dtype)
    greet(peers)
    copies = start_to(peers, lambda peer: outgoing.at[peer["col"]], arrived.at[me], send, recv)
    total = part_ref[:, pl.ds(pl.multiple_of(me * width, width), width)]
    for copy in copies:
        copy.wait()
    for peer in peers:
        total = total + arrived[peer["col"]].astype(jnp.float32)
    return total


def share_kernel_sum(n, part_ref, total_ref, arrived, send, recv):
    me = lax.axis_index("col")
    peers = col_peers(n)
    size = total_ref.shape[0]

    def share(at):
        return pl.ds(pl.multiple_of(at * size, size), size)

    greet(peers)
    copies = start_to(
        peers, lambda peer: part_ref.at[share(peer["col"])], arrived.at[me], send, recv
    )
    arrived[me] = part_ref[share(me), :]
    for copy in copies:
        copy.wait()
    total = arrived[0]
    for k in range(1, n):
        total = total + arrived[k]
    total_ref[...] = total


def share_sum(part):
    n = lax.axis_size("col")
    shape = (part.shape[0] // n, part.shape[1])
    return pl.pallas_call(
        functools.partial(share_kernel_sum, n),
        out_shape=jax.ShapeDtypeStruct(shape, jnp.float32),
        in_specs=[VMEM_SPEC],
        out_specs=VMEM_SPEC,
        scratch_shapes=[
            pltpu.VMEM((n,) + shape, jnp.float32),
            pltpu.SemaphoreType.DMA((n - 1,)),
            pltpu.SemaphoreType.DMA((n - 1,)),
        ],
        compiler_params=pltpu.CompilerParams(collective_id=8, has_side_effects=True),
        name="share_sum",
    )(part)


def rows_over_col(n, product, row_own, row_slots, send, recv):
    me = lax.axis_index("col")
    peers = col_peers(n)
    ones = jnp.ones((8, product.shape[1]), jnp.float32)
    sums = lax.dot_general(
        ones, product, (((1,), (1,)), ((), ())), precision=HIGHEST,
        preferred_element_type=jnp.float32,
    )
    row_own[...] = sums
    row_slots[me] = sums
    copies = start_to(peers, lambda peer: row_own, row_slots.at[me], send, recv)
    for copy in copies:
        copy.wait()
    total = row_slots[0]
    for k in range(1, n):
        total = total + row_slots[k]
    return jnp.transpose(total)[:, :1]


def gather_cols(n, own, all_ref, send, recv):
    me = lax.axis_index("col")
    peers = col_peers(n)
    width = own.shape[1]
    place = all_ref.at[:, pl.ds(pl.multiple_of(me * width, width), width)]
    place[...] = own[...]
    copies = start_to(peers, lambda peer: own, place, send, recv)
    for copy in copies:
        copy.wait()


def forward_turn_kernel(
    n, part_ref, resid_ref, gain_ref, resid_out, scale_out, normed_out,
    outgoing, arrived, row_own, row_slots, own, *sems,
):
    resid = resid_ref[...] + scatter_sum(n, part_ref, outgoing, arrived, sems[0], sems[1])
    resid_out[...] = resid
    square = rows_over_col(n, resid * resid, row_own, row_slots, sems[2], sems[3])
    scale = lax.rsqrt(square / (n * resid.shape[1]) + EPSILON)
    scale_out[...] = scale
    own[...] = (resid * scale * gain_ref[...]).astype(jnp.bfloat16)
    gather_cols(n, own, normed_out, sems[4], sems[5])


def backward_turn_kernel(
    n, spread, part_ref, grad_ref, resid_ref, scale_ref, gain_ref, grad_out, gain_out, *rest
):
    if spread:
        cot_out, rest = rest[0], rest[1:]
    outgoing, arrived, row_own, row_slots, own = rest[:5]
    sems = rest[5:]
    d_normed = scatter_sum(n, part_ref, outgoing, arrived, sems[0], sems[1])
    resid = resid_ref[...]
    scale = scale_ref[...]
    scaled_in = d_normed * gain_ref[...]
    gain_out[...] = jnp.sum(d_normed * resid * scale, axis=0, keepdims=True)
    total = rows_over_col(n, scaled_in * resid, row_own, row_slots, sems[2], sems[3])
    grad = (
        grad_ref[...]
        + scale * scaled_in
        - resid * (scale * scale * scale * total / (n * resid.shape[1]))
    )
    grad_out[...] = grad
    if spread:
        own[...] = grad.astype(jnp.bfloat16)
        gather_cols(n, own, cot_out, sems[4], sems[5])


def turn_scratch(n, rows, width):
    return [
        pltpu.VMEM((n, rows, width), jnp.bfloat16),
        pltpu.VMEM((n, rows, width), jnp.bfloat16),
        pltpu.VMEM((8, rows), jnp.float32),
        pltpu.VMEM((n, 8, rows), jnp.float32),
        pltpu.VMEM((rows, width), jnp.bfloat16),
    ] + [pltpu.SemaphoreType.DMA((n - 1,)) for _ in range(6)]


def forward_turn(part, resid, gain):
    n = lax.axis_size("col")
    rows, width = resid.shape
    return pl.pallas_call(
        functools.partial(forward_turn_kernel, n),
        out_shape=[
            jax.ShapeDtypeStruct((rows, width), jnp.float32),
            jax.ShapeDtypeStruct((rows, 1), jnp.float32),
            jax.ShapeDtypeStruct((rows, n * width), jnp.bfloat16),
        ],
        in_specs=[VMEM_SPEC] * 3,
        out_specs=[VMEM_SPEC] * 3,
        scratch_shapes=turn_scratch(n, rows, width),
        compiler_params=pltpu.CompilerParams(collective_id=1, has_side_effects=True),
        name="forward_turn",
    )(part, resid, gain[None, :])


def backward_turn(part, grad, resid, scale, gain, spread):
    n = lax.axis_size("col")
    rows, width = resid.shape
    outs = [
        jax.ShapeDtypeStruct((rows, width), jnp.float32),
        jax.ShapeDtypeStruct((1, width), jnp.float32),
    ]
    if spread:
        outs.append(jax.ShapeDtypeStruct((rows, n * width), jnp.bfloat16))
    return pl.pallas_call(
        functools.partial(backward_turn_kernel, n, spread),
        out_shape=outs,
        in_specs=[VMEM_SPEC] * 5,
        out_specs=[VMEM_SPEC] * len(outs),
        scratch_shapes=turn_scratch(n, rows, width),
        compiler_params=pltpu.CompilerParams(
            collective_id=2 if spread else 3, has_side_effects=True
        ),
        name="backward_turn" if spread else "backward_end",
    )(part, grad, resid, scale[:, None], gain[None, :])


def entry_kernel(n, tok_ref, gain_ref, tok_all, gain_all, *sems):
    me = lax.axis_index("col")
    peers = col_peers(n)
    width = tok_ref.shape[1]
    place = tok_all.at[:, pl.ds(pl.multiple_of(me * width, width), width)]
    place[...] = tok_ref[...]
    gain_all[me] = gain_ref[...]
    greet(peers)
    copies = start_to(peers, lambda peer: tok_ref, place, sems[0], sems[1])
    copies += start_to(peers, lambda peer: gain_ref, gain_all.at[me], sems[2], sems[3])
    for copy in copies:
        copy.wait()


def entry_gather(tokens, gain):
    n = lax.axis_size("col")
    rows, width = tokens.shape
    return pl.pallas_call(
        functools.partial(entry_kernel, n),
        out_shape=[
            jax.ShapeDtypeStruct((rows, n * width), tokens.dtype),
            jax.ShapeDtypeStruct((n, 1, width), gain.dtype),
        ],
        in_specs=[VMEM_SPEC] * 2,
        out_specs=[VMEM_SPEC] * 2,
        scratch_shapes=[pltpu.SemaphoreType.DMA((n - 1,)) for _ in range(4)],
        compiler_params=pltpu.CompilerParams(collective_id=4, has_side_effects=True),
        name="entry_gather",
    )(tokens, gain[None, :])


def start_pair(src, dst, sems, at, peer):
    copy = pltpu.make_async_remote_copy(
        src_ref=src,
        dst_ref=dst,
        send_sem=sems[0].at[at],
        recv_sem=sems[1].at[at],
        device_id=peer,
        device_id_type=MESH,
    )
    copy.start()
    return copy


def load_kernel(n, axes, tok_ref, cot_ref, gain_ref, *rest):
    count = len(axes)
    weights, rest = rest[:count], rest[count:]
    tok_all, cot_all, gain_all = rest[:3]
    wholes, rest = rest[3 : 3 + count * LAYERS], rest[3 + count * LAYERS :]
    col_sems, across, beside, here = rest[:6], rest[6:8], rest[8:10], rest[10]
    me, at_row, at_dp = lax.axis_index("col"), lax.axis_index("row"), lax.axis_index("dp")
    core = lax.rem(at_dp, 2)
    peers = col_peers(n)
    over = {"row": 1 - at_row}
    twin = {"dp": at_dp + 1 - 2 * core}
    width = tok_ref.shape[1]
    columns = pl.ds(pl.multiple_of(me * width, width), width)
    tok_place, cot_place = tok_all.at[:, columns], cot_all.at[:, columns]
    tok_place[...] = tok_ref[...]
    cot_place[...] = cot_ref[...]
    gain_all[me] = gain_ref[...]
    greet(peers + [over, twin])

    def part(ref, axis, start, size):
        window = pl.ds(pl.multiple_of(start, size), size)
        return ref.at[window] if axis == 0 else ref.at[:, window]

    copies = start_to(peers, lambda peer: tok_ref, tok_place, col_sems[0], col_sems[1])
    copies += start_to(peers, lambda peer: gain_ref, gain_all.at[me], col_sems[2], col_sems[3])
    jobs = []
    for layer_at in range(LAYERS):
        for slot, axis in enumerate(axes):
            at = layer_at * count + slot
            block, whole = weights[slot].at[layer_at], wholes[at]
            size = block.shape[axis]
            half = size // 2
            sent = start_pair(
                part(block, axis, core * half, half),
                part(whole, axis, at_row * size + core * half, half),
                across,
                at,
                over,
            )
            kept = pltpu.make_async_copy(
                block, part(whole, axis, at_row * size, size), here.at[at]
            )
            kept.start()
            jobs.append((sent, kept, whole, axis, size, half))
    copies += start_to(peers, lambda peer: cot_ref, cot_place, col_sems[4], col_sems[5])
    passed = []
    for at, (sent, kept, whole, axis, size, half) in enumerate(jobs):
        sent.wait_recv()
        landed = part(whole, axis, (1 - at_row) * size + core * half, half)
        passed.append(start_pair(landed, landed, beside, at, twin))
    for sent, kept, *unused in jobs:
        sent.wait_send()
        kept.wait()
    for copy in passed + copies:
        copy.wait()


def load_all(tokens, cotangent, gain, weights, axes):
    n = lax.axis_size("col")
    rows, width = tokens.shape
    outs = [
        jax.ShapeDtypeStruct((rows, n * width), tokens.dtype),
        jax.ShapeDtypeStruct((rows, n * width), cotangent.dtype),
        jax.ShapeDtypeStruct((n, 1, width), gain.dtype),
    ]
    for layer_at in range(LAYERS):
        for weight, axis in zip(weights, axes):
            shape = list(weight.shape[1:])
            shape[axis] *= 2
            outs.append(jax.ShapeDtypeStruct(tuple(shape), weight.dtype))
    count = len(weights) * LAYERS
    return pl.pallas_call(
        functools.partial(load_kernel, n, axes),
        out_shape=outs,
        in_specs=[VMEM_SPEC] * (3 + len(weights)),
        out_specs=[VMEM_SPEC] * (3 + count),
        scratch_shapes=[pltpu.SemaphoreType.DMA((n - 1,)) for _ in range(6)]
        + [pltpu.SemaphoreType.DMA((count,)) for _ in range(5)],
        compiler_params=pltpu.CompilerParams(collective_id=7, has_side_effects=True, vmem_limit_bytes=40 * 2**20),
        name="load_all",
    )(tokens, cotangent, gain[None, :], *weights)


def small_kernel(dp, row, value_ref, total_ref, slots, send, recv):
    at_dp, at_row = lax.axis_index("dp"), lax.axis_index("row")
    me = at_dp * row + at_row
    peers = []
    for k in range(1, dp * row):
        peers.append(
            {"dp": lax.rem(at_dp + k // row, dp), "row": lax.rem(at_row + k % row, row)}
        )
    slots[me] = value_ref[...]
    greet(peers)
    copies = start_to(peers, lambda peer: value_ref, slots.at[me], send, recv)
    for copy in copies:
        copy.wait()
    total = slots[0]
    for k in range(1, dp * row):
        total = total + slots[k]
    total_ref[...] = total


def small_total(value):
    dp, row = lax.axis_size("dp"), lax.axis_size("row")
    count = dp * row
    if count > 8:
        return lax.psum(value, ("dp", "row"))
    return pl.pallas_call(
        functools.partial(small_kernel, dp, row),
        out_shape=jax.ShapeDtypeStruct(value.shape, jnp.float32),
        in_specs=[VMEM_SPEC],
        out_specs=VMEM_SPEC,
        scratch_shapes=[
            pltpu.VMEM((count,) + value.shape, jnp.float32),
            pltpu.SemaphoreType.DMA((count - 1,)),
            pltpu.SemaphoreType.DMA((count - 1,)),
        ],
        compiler_params=pltpu.CompilerParams(collective_id=5, has_side_effects=True),
        name="small_total",
    )(value)


def whole_over_row(block, axis):
    if lax.axis_size("row") != 2:
        return lax.all_gather(block, "row", axis=axis, tiled=True)
    other = lax.ppermute(block, "row", [(0, 1), (1, 0)])
    size = block.shape[axis]
    trio = jnp.concatenate([block, other, block], axis=axis)
    return lax.dynamic_slice_in_dim(trio, lax.axis_index("row") * size, 2 * size, axis)


def whole_over_col(block):
    n = lax.axis_size("col")
    size = block.shape[1]
    blocks = [block]
    for k in range(1, n):
        blocks.append(lax.ppermute(block, "col", [(i, (i - k) % n) for i in range(n)]))
    twice = jnp.concatenate(blocks + blocks[:-1], axis=1)
    start = lax.rem(n - lax.axis_index("col"), n) * size
    return lax.dynamic_slice_in_dim(twice, start, n * size, 1)


def packed_small(parts):
    flat = jnp.concatenate([part.reshape(-1) for part in parts])
    total = flat.shape[0]
    lines = -(-total // 1024) * 8
    return jnp.pad(flat, (0, lines * 128 - total)).reshape(lines, 128)


def unpacked_small(packed, shapes):
    flat = packed.reshape(-1)
    out, at = [], 0
    for shape in shapes:
        size = 1
        for extent in shape:
            size *= extent
        out.append(flat[at : at + size].reshape(shape))
        at += size
    return out


def link_up(earlier, later):
    return (earlier[0] * later[0], later[0][:, None, None] * earlier[1] + later[1])


def link_down(earlier, later):
    return (earlier[0] * later[0], later[1] + later[0][:, None, None] * earlier[1])


def mixer_parts(
    post_x, b_mat, c_mat, raw_step, step_off, decay_rate, skip_rate, segments, seg_prior
):
    tok_count = post_x.shape[0]
    head_count = raw_step.shape[1]
    head_width = post_x.shape[1] // head_count
    block_count = tok_count // SPAN
    step_size = jax.nn.softplus(raw_step + step_off[None, :])
    decay_now = -jnp.exp(decay_rate)[None, :] * step_size
    xs_c = post_x.reshape(block_count, SPAN, head_count, head_width)
    step_c = step_size.reshape(block_count, SPAN, head_count)
    cumulative = jnp.cumsum(decay_now.reshape(block_count, SPAN, head_count), axis=1)
    b_c = b_mat.reshape(block_count, SPAN, -1)
    c_c = c_mat.reshape(block_count, SPAN, -1)
    seg_c = segments.reshape(block_count, SPAN)
    places = jnp.arange(SPAN)
    same_seq = (seg_c[:, :, None] == seg_c[:, None, :]) & (places[:, None] >= places[None, :])[None]
    causal = same_seq.astype(jnp.float32)[:, None, :, :]
    cum_heads = jnp.transpose(cumulative, (0, 2, 1))
    step_heads = jnp.transpose(step_c, (0, 2, 1))
    spread = cum_heads[:, :, :, None] - cum_heads[:, :, None, :]
    scores = jnp.einsum("cin,cjn->cij", c_c, b_c, precision=HIGHEST)
    weights = jnp.exp(spread * causal) * causal * scores[:, None, :, :] * step_heads[:, :, None, :]
    intra_part = jnp.einsum("chij,cjhp->cihp", weights, xs_c, precision=HIGHEST)
    entry_gate = jnp.exp(cumulative) * (seg_c == seg_prior[:, None]).astype(jnp.float32)[..., None]
    tail_gate = (
        jnp.exp(cumulative[:, -1:, :] - cumulative)
        * (seg_c == seg_c[:, -1:]).astype(jnp.float32)[..., None]
        * step_c
    )
    fresh_state = jnp.einsum("cjh,cjhp,cjn->chpn", tail_gate, xs_c, b_c, precision=HIGHEST)
    block_decay = (
        jnp.exp(cumulative[:, -1, :]) * (seg_c[:, -1] == seg_prior).astype(jnp.float32)[:, None]
    )

    def advance(state_now, element):
        return (element[1][:, None, None] * state_now + element[0], state_now)

    dev_state, starts = lax.scan(
        advance, jnp.zeros_like(fresh_state[0]), (fresh_state, block_decay)
    )
    prefix = jnp.cumprod(
        jnp.concatenate([jnp.ones_like(block_decay), block_decay[:-1]], axis=0), axis=0
    )
    dev_decay = prefix[-1] * block_decay[-1]
    local_part = intra_part + skip_rate[None, None, :, None] * xs_c
    return (local_part, entry_gate, c_c, starts, prefix, dev_state, dev_decay)


def mixer_finish(pieces, entry_state):
    local_part, entry_gate, c_c, starts, prefix, dev_state, dev_decay = pieces
    states = starts + prefix[:, :, None, None] * entry_state[None]
    incoming = jnp.einsum("chpn,cin->cihp", states, c_c, precision=HIGHEST)
    mixed_out = local_part + entry_gate[..., None] * incoming
    return mixed_out.reshape(mixed_out.shape[0] * SPAN, -1)


def mixer_core(
    post_x,
    b_mat,
    c_mat,
    raw_step,
    step_off,
    decay_rate,
    skip_rate,
    entry_state,
    segments,
    seg_prior,
):
    pieces = mixer_parts(
        post_x, b_mat, c_mat, raw_step, step_off, decay_rate, skip_rate, segments, seg_prior
    )
    return (mixer_finish(pieces, entry_state), pieces[5], pieces[6])


def local(
    tokens,
    segment_index,
    cotangent,
    norm_gain,
    gate_weight,
    inner_weight,
    state_weight,
    step_weight,
    inner_kernel,
    inner_bias,
    state_kernel,
    state_bias,
    step_bias,
    decay_log,
    skip_gain,
    gated_gain,
    output_weight,
):
    tok_rows = tokens.shape[0]
    full_width = tokens.shape[1] * lax.axis_size("col")
    head_count = step_bias.shape[1]
    inner_cols = inner_kernel.shape[1]
    inner_full = inner_cols * lax.axis_size("col")
    state_cols = state_kernel.shape[1]
    state_half = state_cols // 2
    share_cols = state_cols // lax.axis_size("col")
    col_at = lax.axis_index("col")
    first_tok = lax.axis_index("row") * tok_rows
    group_seg = segment_index[0]
    seg_front = jnp.concatenate([jnp.full((KERNEL - 1,), -1, jnp.int32), group_seg])
    seg_rear = jnp.concatenate([group_seg, jnp.full((KERNEL - 1,), -2, jnp.int32)])
    seg_early = lax.dynamic_slice_in_dim(seg_front, first_tok, tok_rows + KERNEL - 1)
    seg_late = lax.dynamic_slice_in_dim(seg_rear, first_tok, tok_rows + KERNEL - 1)
    segments = seg_early[KERNEL - 1 :]
    seg_prior = jnp.concatenate(
        [seg_early[KERNEL - 2 : KERNEL - 1], segments[SPAN - 1 : -1 : SPAN]]
    )
    dims_t = (((1,), (1,)), ((), ()))
    dims_w = (((0,), (0,)), ((), ()))
    resid = tokens.astype(jnp.float32)
    paired = lax.axis_size("row") == 2 and lax.axis_size("dp") % 2 == 0
    if paired:
        tokens_all, cot_all, gain_all, *wholes = load_all(
            tokens,
            cotangent,
            norm_gain[0],
            (gate_weight, inner_weight, state_weight, output_weight),
            (0, 0, 0, 1),
        )
    else:
        tokens_all, gain_all = entry_gather(tokens, norm_gain[0])
        cot_all = whole_over_col(cotangent)
    first_all = tokens_all.astype(jnp.float32)
    row_scale = lax.rsqrt(jnp.sum(first_all * first_all, axis=1) / full_width + EPSILON)
    normed_all = (first_all * row_scale[:, None] * gain_all.reshape(1, -1)).astype(jnp.bfloat16)
    whole_weights = []
    for layer_at in range(LAYERS):
        step_full = whole_over_row(step_weight[layer_at], 0)
        if paired:
            gate_full, inner_whole, state_full, output_full = wholes[
                4 * layer_at : 4 * layer_at + 4
            ]
        else:
            gate_full = whole_over_row(gate_weight[layer_at], 0)
            inner_whole = whole_over_row(inner_weight[layer_at], 0)
            state_full = whole_over_row(state_weight[layer_at], 0)
            output_full = whole_over_row(output_weight[layer_at], 1)
        whole_weights.append((gate_full, inner_whole, state_full, step_full, output_full))
    saved = []
    for layer_at in range(LAYERS):
        gate_full, inner_whole, state_full, step_full, output_full = whole_weights[layer_at]
        gate_val = jnp.dot(normed_all, gate_full, preferred_element_type=jnp.float32)
        inner_val = jnp.dot(normed_all, inner_whole, preferred_element_type=jnp.float32)
        pair_val = jnp.dot(normed_all, state_full, preferred_element_type=jnp.float32)
        raw_step = jnp.dot(normed_all, step_full, preferred_element_type=jnp.float32)
        values = jnp.concatenate([inner_val, pair_val], axis=1)
        before = passed_along(values[tok_rows - (KERNEL - 1) :], "row", 1)
        padded = jnp.concatenate([before, values], axis=0)
        kernels = jnp.concatenate([inner_kernel[layer_at], state_kernel[layer_at]], axis=0)
        pre_act = (
            jnp.zeros_like(values)
            + jnp.concatenate([inner_bias[layer_at], state_bias[layer_at]])[None, :]
        )
        for offset in range(KERNEL):
            same_seq = (seg_early[offset : offset + tok_rows] == segments).astype(jnp.float32)
            pre_act = (
                pre_act
                + kernels[:, offset][None, :]
                * padded[offset : offset + tok_rows]
                * same_seq[:, None]
            )
        post_act = jax.nn.silu(pre_act)
        post_x = post_act[:, :inner_cols]
        b_mat = post_act[:, inner_cols : inner_cols + state_half]
        c_mat = post_act[:, inner_cols + state_half :]
        pieces = mixer_parts(
            post_x,
            b_mat,
            c_mat,
            raw_step,
            step_bias[layer_at],
            decay_log[layer_at],
            skip_gain[layer_at],
            segments,
            seg_prior,
        )
        unused, entry_state = carried_in(
            (pieces[6], pieces[5]),
            "row",
            link_up,
            (jnp.ones_like(pieces[6]), jnp.zeros_like(pieces[5])),
            False,
        )
        mixed_out = mixer_finish(pieces, entry_state)
        silu_gate = jax.nn.silu(gate_val)
        gated = mixed_out * silu_gate
        power_part = jnp.sum(gated * gated, axis=1)
        if layer_at + 1 < LAYERS:
            power_sum = row_total(power_part[None, :])[0]
        else:
            last_dyn = lax.dot_general(
                cot_all, output_full, dims_t, preferred_element_type=jnp.float32
            )
            last_scaled = last_dyn * gated_gain[layer_at][None, :]
            power_sum, last_total = row_total(
                jnp.stack([power_part, jnp.sum(last_scaled * gated, axis=1)], axis=0)
            )
        gated_scale = lax.rsqrt(power_sum / inner_full + EPSILON)
        normed_y = (gated * gated_scale[:, None] * gated_gain[layer_at][None, :]).astype(
            jnp.bfloat16
        )
        partial_out = jnp.dot(normed_y, output_full, preferred_element_type=jnp.float32)
        stored = None
        saved.append(
            (
                resid,
                row_scale,
                normed_all,
                gate_val,
                padded,
                pre_act,
                post_x,
                b_mat,
                c_mat,
                raw_step,
                entry_state,
                pieces[4],
                pieces[1],
                pieces[6],
                mixed_out,
                silu_gate,
                gated,
                gated_scale,
                normed_y,
                stored,
            )
        )
        if layer_at + 1 < LAYERS:
            resid, new_scale, normed_all = forward_turn(
                partial_out, resid, norm_gain[layer_at + 1]
            )
            row_scale = new_scale[:, 0]
        else:
            resid = resid + lax.psum_scatter(partial_out, "col", scatter_dimension=1, tiled=True)
    layer_output = resid.astype(jnp.bfloat16)
    resid_grad = cotangent.astype(jnp.float32)
    big_grads = [None] * LAYERS
    small_terms = [None] * LAYERS
    for layer_at in reversed(range(LAYERS)):
        (
            resid,
            row_scale,
            normed_all,
            gate_val,
            padded,
            pre_act,
            post_x,
            b_mat,
            c_mat,
            raw_step,
            entry_state,
            prefix,
            entry_gate,
            dev_decay,
            mixed_out,
            silu_gate,
            gated,
            gated_scale,
            normed_y,
            stored,
        ) = saved[layer_at]
        gate_full, inner_whole, state_full, step_full, output_full = whole_weights[layer_at]
        if layer_at + 1 < LAYERS:
            d_normed_y = lax.dot_general(
                cot_all, output_full, dims_t, preferred_element_type=jnp.float32
            )
        else:
            d_normed_y = last_dyn
        grad_out = lax.dot_general(cot_all, normed_y, dims_w, preferred_element_type=jnp.float32)
        scaled_y = d_normed_y * gated_gain[layer_at][None, :]
        if layer_at + 1 < LAYERS:
            total_y = row_total(jnp.sum(scaled_y * gated, axis=1)[None, :])[0]
        else:
            total_y = last_total
        d_gated = (
            gated_scale[:, None] * scaled_y
            - gated * (gated_scale**3 * total_y / inner_full)[:, None]
        )
        gain_y = jnp.sum(d_normed_y * gated * gated_scale[:, None], axis=0)
        d_mixed = d_gated * silu_gate
        sigma_gate = jax.nn.sigmoid(gate_val)
        d_gate = d_gated * mixed_out * sigma_gate * (1.0 + gate_val * (1.0 - sigma_gate))
        block_count = tok_rows // SPAN
        d_mixed_c = d_mixed.reshape(block_count, SPAN, head_count, -1)
        c_blocks = c_mat.reshape(block_count, SPAN, -1)
        reach_gate = prefix[:, None, :] * entry_gate
        local_pull = jnp.einsum(
            "cih,cihp,cin->hpn", reach_gate, d_mixed_c, c_blocks, precision=HIGHEST
        )
        unused_b, state_pull = carried_in(
            (dev_decay, local_pull),
            "row",
            link_down,
            (jnp.ones_like(dev_decay), jnp.zeros_like(local_pull)),
            True,
        )
        decay_pull = jnp.sum(state_pull * entry_state, axis=(1, 2))

        def local_mixer(px_val, bm_val, cm_val, rs_val, so_val, dr_val, sr_val, es_val):
            return mixer_core(
                px_val, bm_val, cm_val, rs_val, so_val, dr_val, sr_val, es_val, segments, seg_prior
            )

        unused_c, pullback = jax.vjp(
            local_mixer,
            post_x,
            b_mat,
            c_mat,
            raw_step,
            step_bias[layer_at],
            decay_log[layer_at],
            skip_gain[layer_at],
            entry_state,
        )
        d_post_x, grad_b, grad_c, d_raw_step, g_step_bias, g_decay, g_skip, unused_d = pullback(
            (d_mixed, state_pull, decay_pull)
        )
        d_share = share_sum(jnp.concatenate([grad_b.T, grad_c.T], axis=0)).T
        d_post = jnp.concatenate([d_post_x, d_share], axis=1)
        share_pre = lax.dynamic_slice_in_dim(
            pre_act[:, inner_cols:], col_at * share_cols, share_cols, 1
        )
        own_pre = jnp.concatenate([pre_act[:, :inner_cols], share_pre], axis=1)
        sigma_pre = jax.nn.sigmoid(own_pre)
        d_pre = d_post * sigma_pre * (1.0 + own_pre * (1.0 - sigma_pre))
        after_rows = passed_along(d_pre[: KERNEL - 1], "row", -1)
        d_pre_ext = jnp.concatenate([d_pre, after_rows], axis=0)
        share_kernel = lax.dynamic_slice_in_dim(
            state_kernel[layer_at], col_at * share_cols, share_cols, 0
        )
        own_kernel = jnp.concatenate([inner_kernel[layer_at], share_kernel], axis=0)
        share_padded = lax.dynamic_slice_in_dim(
            padded[:, inner_cols:], col_at * share_cols, share_cols, 1
        )
        own_padded = jnp.concatenate([padded[:, :inner_cols], share_padded], axis=1)
        d_values = jnp.zeros_like(d_pre)
        kernel_terms = []
        for offset in range(KERNEL):
            lead_by = KERNEL - 1 - offset
            same_back = (seg_late[lead_by : lead_by + tok_rows] == segments).astype(jnp.float32)
            d_values = (
                d_values
                + own_kernel[:, offset][None, :]
                * d_pre_ext[lead_by : lead_by + tok_rows]
                * same_back[:, None]
            )
            same_fwd = (seg_early[offset : offset + tok_rows] == segments).astype(jnp.float32)
            kernel_terms.append(
                jnp.sum(d_pre * own_padded[offset : offset + tok_rows] * same_fwd[:, None], axis=0)
            )
        kernel_grad = jnp.stack(kernel_terms, axis=0)
        bias_grad = jnp.sum(d_pre, axis=0)
        d_gate16 = d_gate.astype(jnp.bfloat16)
        d_inner16 = d_values[:, :inner_cols].astype(jnp.bfloat16)
        d_pair16 = d_values[:, inner_cols:].astype(jnp.bfloat16)
        d_step16 = d_raw_step.astype(jnp.bfloat16)
        share_weight = lax.dynamic_slice_in_dim(state_full, col_at * share_cols, share_cols, 1)
        partial_in = lax.dot_general(
            d_gate16, gate_full, dims_t, preferred_element_type=jnp.float32
        )
        partial_in = partial_in + lax.dot_general(
            d_inner16, inner_whole, dims_t, preferred_element_type=jnp.float32
        )
        partial_in = partial_in + lax.dot_general(
            d_pair16, share_weight, dims_t, preferred_element_type=jnp.float32
        )
        partial_in = partial_in + lax.dot_general(
            d_step16, step_full, dims_t, preferred_element_type=jnp.float32
        )
        low_grads = jnp.concatenate([d_gate16, d_inner16, d_pair16, d_step16], axis=1)
        low_grads = jnp.pad(low_grads, ((0, 0), (0, -low_grads.shape[1] % 128)))
        grad_in = lax.dot_general(normed_all, low_grads, dims_w, preferred_element_type=jnp.float32)
        layer_grads = jnp.concatenate(
            [grad_out.astype(jnp.bfloat16), grad_in.astype(jnp.bfloat16)], axis=1
        )
        if layer_at > 0:
            layer_grads, partial_in = lax.optimization_barrier((layer_grads, partial_in))
        big_grads[layer_at] = lax.psum_scatter(
            layer_grads, ("dp", "row"), scatter_dimension=0, tiled=True
        ).astype(jnp.float32)
        turned = backward_turn(
            partial_in, resid_grad, resid, row_scale, norm_gain[layer_at], layer_at > 0
        )
        resid_grad, gain_in = turned[0], turned[1][0]
        if layer_at > 0:
            cot_all = turned[2]
        small_terms[layer_at] = (
            gain_in,
            gain_y,
            kernel_grad[:, :inner_cols],
            bias_grad[:inner_cols],
            kernel_grad[:, inner_cols:],
            bias_grad[inner_cols:],
            g_step_bias,
            g_decay,
            g_skip,
        )

    model_cols = output_weight.shape[1]
    sizes = (model_cols, inner_cols, inner_cols, share_cols, head_count)
    summed, at = [], 0
    for size in sizes:
        summed.append(jnp.stack([big[:, at : at + size] for big in big_grads], axis=0))
        at += size
    shapes = [part.shape for terms in small_terms for part in terms]
    unpacked = unpacked_small(
        small_total(packed_small([part for terms in small_terms for part in terms])), shapes
    )
    count = len(small_terms[0])
    smalls = [
        jnp.stack([unpacked[layer_at * count + slot] for layer_at in range(LAYERS)], axis=0)
        for slot in range(count)
    ]
    return (
        layer_output,
        resid_grad,
        smalls[0],
        summed[1],
        summed[2],
        summed[3],
        summed[4],
        jnp.swapaxes(smalls[2], 1, 2),
        smalls[3],
        jnp.swapaxes(smalls[4], 1, 2),
        smalls[5],
        smalls[6],
        smalls[7],
        smalls[8],
        smalls[1],
        jnp.transpose(summed[0], (0, 2, 1)),
    )


def solution(mesh):
    placed = (
        P(("dp", "row"), "col"),
        P("dp", None),
        P(("dp", "row"), "col"),
        P(None, "col"),
        P(None, "row", "col"),
        P(None, "row", "col"),
        P(None, "row", None),
        P(None, "row", "col"),
        P(None, "col", None),
        P(None, "col"),
        P(),
        P(),
        P(None, "col"),
        P(None, "col"),
        P(None, "col"),
        P(None, "col"),
        P(None, "col", "row"),
    )
    return jax.shard_map(
        local,
        mesh=mesh,
        in_specs=placed,
        out_specs=(
            P(("dp", "row"), "col"),
            P(("dp", "row"), "col"),
            P(None, "col"),
            P(None, ("dp", "row"), "col"),
            P(None, ("dp", "row"), "col"),
            P(None, ("dp", "row"), "col"),
            P(None, ("dp", "row"), "col"),
            P(None, "col", None),
            P(None, "col"),
            P(None, "col", None),
            P(None, "col"),
            P(None, "col"),
            P(None, "col"),
            P(None, "col"),
            P(None, "col"),
            P(None, "col", ("dp", "row")),
        ),
        check_vma=False,
    )
```
